256 devices in a mesh: tok: 64 (over x, z, core), feat: 4 (over y).
Axes of the slice: x: 4, y: 4, z: 8, core: 2. Of those that a mesh axis runs over, the one named last changes fastest.
Arguments:
- queries: bfloat16 [8192, 4096], P('tok', 'feat'), may hold values from -12 to 12
- keys: bfloat16 [8192, 1024], P('tok', 'feat'), may hold values from -12 to 12
- values: bfloat16 [8192, 1024], P('tok', 'feat'), may hold values from -6 to 6
- out_weight: bfloat16 [4096, 4096], P('feat', 'tok'), may hold values from -0.09375 to 0.09375
- doc_lengths: int32 [6], replicated, may hold values from 1 to 5120, 8192 in all
Outputs:
- mixed: bfloat16 [8192, 4096], P('tok', 'feat')
The draws below stay inside these ranges and needn't reach their ends.
Inputs may be any that keep to these rules, and one draw needn't show every extreme that they name: `doc_lengths`: the lengths sum to 8192, and the largest is exactly 5120.
All inputs are finite; a program needn't handle non-finite values.
Results may differ from the reference program's by a relative error of at most 0.012.
The reference program's roundings to bfloat16 on the way count: a program that leaves them out, or rounds other values in their place, can miss the bound.
Values may be sent and summed in bfloat16 or wider, within the bound.
A program may use at most 64 MiB of HBM per device.

```python
import math
import jax
import jax.numpy as jnp
import numpy as np
from jax import lax

QH = 32
KVH = 8
HD = 128
D = 4096
DOCS = 6
TOKENS = 8192
MOST = 5120
N_FEAT = 4


def draw_queries(key, part):
    normal_part = 2.0 * jnp.clip(jax.random.normal(jax.random.fold_in(key, 1), (TOKENS, QH, HD), jnp.float32), -6.0, 6.0)
    return normal_part.reshape(TOKENS, QH * HD).astype(jnp.bfloat16)


def draw_keys(key, part):
    normal_part = 1.5 * jnp.clip(jax.random.normal(jax.random.fold_in(key, 2), (TOKENS, KVH, HD), jnp.float32), -6.0, 6.0)
    return normal_part.reshape(TOKENS, KVH * HD).astype(jnp.bfloat16)


def steps_of(own_key, extent, split, least, high):
    level = 1.0
    for position, shards_of in split:
        heights = jax.random.uniform(jax.random.fold_in(jax.random.fold_in(own_key, 6), position), (shards_of,), jnp.float32, least / len(split), high / len(split))
        level = level * jnp.repeat(jnp.exp(heights), extent[position] // shards_of).reshape((-1,) + (1,) * (len(extent) - 1 - position))
    return level


def profile(count, total, bound, lean):
    portions = [(1 << 20) // math.isqrt(grade ** lean) + 1 for grade in range(2, count + 1)]
    surplus, given = total - bound - (count - 1), [1] * (count - 1)
    while surplus > 0:
        free = [i for i in range(count - 1) if given[i] < bound]
        whole, remaining = sum([portions[i] for i in free]), surplus
        for i in free:
            more = min(bound - given[i], max(1, remaining * portions[i] // whole), surplus)
            given[i] = given[i] + more
            surplus = surplus - more
    return np.array([bound] + given)


def uneven(stream_key, number_of, total, most, skew):
    if number_of == 2:
        one = jax.random.randint(stream_key, (), max(1, total - most), min(most, total - 1) + 1)
        return jnp.stack([one, total - one])
    sizes = jnp.asarray(profile(number_of, total, most, skew), jnp.int32)
    twos = (number_of - 1) // 2
    donor, sink = sizes[1:1 + 2 * twos:2], sizes[2:2 + 2 * twos:2]
    room = jnp.minimum(donor - 1, most - sink)
    passed = jax.random.randint(jax.random.fold_in(stream_key, 1), (twos,), 0, 1 << 20) % (room + 1)
    sizes = sizes.at[1:1 + 2 * twos:2].set(donor - passed).at[2:2 + 2 * twos:2].set(sink + passed)
    return sizes[jax.random.permutation(jax.random.fold_in(stream_key, 2), number_of)]


def gaussian(key, dims, scale, most, cuts=(), held_as=jnp.bfloat16):
    entries = jax.random.normal(key, dims, jnp.float32) * scale
    if len(cuts) > 0:
        entries = steps_of(key, dims, cuts, -0.22, 0.18) * entries
    return jnp.clip(entries, min=-most, max=most).astype(held_as)


def setup_inputs(seed: int = 0) -> dict:
    key_list = jax.random.split(jax.random.key(seed), 6)
    queries = draw_queries(jax.random.fold_in(key_list[5], 71), 0)
    keys = draw_keys(jax.random.fold_in(key_list[5], 71), 0)
    values = gaussian(key_list[2], (TOKENS, KVH * HD), 1.0, 6.0, ((0, 64), (1, 4)))
    out_weight = gaussian(key_list[3], (D, D), D ** -0.5, 0.09375, ((0, 4), (1, 64)))
    doc_lengths = uneven(key_list[4], DOCS, TOKENS, MOST, 2).astype(jnp.int32)
    return dict(queries=queries, keys=keys, values=values, out_weight=out_weight, doc_lengths=doc_lengths)


ROPE_BASE = 500000.0
NEG_FILL = -1.0e30


def locate(token_index, doc_lengths):
    doc_ends = jnp.cumsum(doc_lengths).astype(jnp.int32)
    starts = doc_ends - doc_lengths
    doc_ids = jnp.sum((token_index[:, None] >= doc_ends[None, :]).astype(jnp.int32), axis=1)
    number = jnp.arange(doc_lengths.shape[0], dtype=jnp.int32)
    first_token = jnp.sum(jnp.where(doc_ids[:, None] == number[None, :], starts[None, :], 0), axis=1)
    return doc_ids, (token_index - first_token).astype(jnp.int32)


def rotary(tensor, positions):
    half_size = tensor.shape[-1] // 2
    frequency = ROPE_BASE ** (-(jnp.arange(half_size, dtype=jnp.float32) * 2.0 / tensor.shape[-1]))
    angles = positions.astype(jnp.float32)[:, None] * frequency[None, :]
    cosine = jnp.cos(angles)[:, None, :]
    sine_part = jnp.sin(angles)[:, None, :]
    first_half = tensor[..., :half_size]
    second_half = tensor[..., half_size:]
    return jnp.concatenate([first_half * cosine - second_half * sine_part, second_half * cosine + first_half * sine_part], axis=-1)


def reference(queries, keys, values, out_weight, doc_lengths):
    token_index = jnp.arange(TOKENS, dtype=jnp.int32)
    doc_ids, positions = locate(token_index, doc_lengths)
    rotated_q = rotary(queries.astype(jnp.float32).reshape(TOKENS, QH, HD), positions).astype(jnp.bfloat16)
    rotated_k = rotary(keys.astype(jnp.float32).reshape(TOKENS, KVH, HD), positions).astype(jnp.bfloat16)
    value_heads = values.reshape(TOKENS, KVH, HD)
    group_size = QH // KVH
    tile_rows = min(256, TOKENS)
    window = min(TOKENS, MOST + tile_rows)
    scale_factor = HD ** -0.5

    def one_tile(block_number):
        first_row = (block_number * tile_rows).astype(jnp.int32)
        query_tile = lax.dynamic_slice_in_dim(rotated_q, first_row, tile_rows, 0)
        query_tile = query_tile.reshape(tile_rows, KVH, group_size, HD).astype(jnp.float32)
        key_first = jnp.clip(first_row + tile_rows - window, 0, TOKENS - window).astype(jnp.int32)
        key_tile = lax.dynamic_slice_in_dim(rotated_k, key_first, window, 0).astype(jnp.float32)
        value_tile = lax.dynamic_slice_in_dim(value_heads, key_first, window, 0).astype(jnp.float32)
        scores = jnp.einsum('qgjd,kgd->gjqk', query_tile, key_tile) * scale_factor
        query_index = first_row + jnp.arange(tile_rows, dtype=jnp.int32)
        key_index = key_first + jnp.arange(window, dtype=jnp.int32)
        query_doc = lax.dynamic_slice_in_dim(doc_ids, first_row, tile_rows, 0)
        key_doc = lax.dynamic_slice_in_dim(doc_ids, key_first, window, 0)
        visible = (query_doc[:, None] == key_doc[None, :]) & (key_index[None, :] <= query_index[:, None])
        scores = jnp.where(visible, scores, NEG_FILL)
        row_max = jnp.max(scores, axis=-1, keepdims=True)
        weights = jnp.where(visible, jnp.exp(scores - row_max), 0.0)
        totals = jnp.sum(weights, axis=-1)
        rounded = lax.optimization_barrier(weights.astype(jnp.bfloat16)).astype(jnp.float32)
        output = jnp.einsum('gjqk,kgd->gjqd', rounded, value_tile) / totals[..., None]
        return output.transpose(2, 0, 1, 3).reshape(tile_rows, QH * HD).astype(jnp.bfloat16)

    attended = lax.map(one_tile, jnp.arange(TOKENS // tile_rows, dtype=jnp.int32))
    attended = attended.reshape(TOKENS, QH * HD)
    block_width = D // N_FEAT
    mixed_sum = jnp.zeros((TOKENS, D), jnp.float32)
    for block_number in range(N_FEAT):
        lower = block_number * block_width
        partial_value = jnp.dot(attended[:, lower:lower + block_width], out_weight[lower:lower + block_width, :], preferred_element_type=jnp.float32)
        partial_value = lax.optimization_barrier(partial_value.astype(jnp.bfloat16)).astype(jnp.float32)
        mixed_sum = mixed_sum + partial_value
    return mixed_sum.astype(jnp.bfloat16)
```

```python
import functools

import jax
import jax.numpy as jnp
import numpy as np
from jax import lax
from jax.experimental import pallas as pl
from jax.experimental.pallas import tpu as pltpu
from jax.sharding import PartitionSpec as P

HD = 128
ROPE_BASE = 500000.0
LOW = -1e30
MASKED = -2e30
ROWS = 128
NX, NZ, NY = 4, 8, 4
FACTOR = float(HD**-0.5 * np.log2(np.e))
MESH = pl.DeviceIdType.MESH


def rotary_tables(doc_lengths):
    token = lax.axis_index("tok") * ROWS + lax.broadcasted_iota(jnp.int32, (ROWS, HD), 0)
    lane = lax.broadcasted_iota(jnp.int32, (ROWS, HD), 1)
    start = jnp.zeros((ROWS, HD), jnp.int32)
    end = jnp.int32(0)
    for number in range(doc_lengths.shape[0]):
        end = end + doc_lengths[number]
        start = jnp.where(token >= end, end, start)
    half = HD // 2
    frequency = (ROPE_BASE ** (-(np.arange(half, dtype=np.float64) * 2.0 / HD))).astype(np.float32)
    both = jnp.asarray(np.concatenate([frequency, frequency]))
    angles = (token - start).astype(jnp.float32) * both[None, :]
    sine = jnp.sin(angles)
    return jnp.cos(angles), jnp.where(lane < half, -sine, sine)


def kernel(
    q_in, k_in, v_in, w_in, cos_in, sin_in, len_ref, out_ref,
    q_stage, kv_stage, qbuf, kv, start_ref, m_ref, l_ref, acc_ref, own_att, att, wbuf, pbuf, part,
    a_s, a_r, q_s, q_r, z_s, z_r, sh_s, sh_r, g_s, g_r, w_s, w_r, wsh_s, wsh_r, e_s, e_r,
):
    t = lax.axis_index("tok")
    y = lax.axis_index("feat")
    x = t // 16
    z = (t // 2) % NZ
    c = t % 2

    def device(dx, dz, dc):
        return (((x + dx) % NX) * 16 + ((z + dz) % NZ) * 2 + (c + dc) % 2, y)

    sibling = device(0, 0, 1)

    barrier = pltpu.get_barrier_semaphore()
    count = 0

    def greet(who):
        pl.semaphore_signal(barrier, inc=1, device_id=who, device_id_type=MESH)

    for dx in range(NX):
        for dy in range(NY):
            if dx or dy:
                greet((((x + dx) % NX) * 16 + z * 2 + c, (y + dy) % NY))
                count += 1
        greet(device(dx, 0, 1))
        count += 1
    for dz in (1, NZ - 1):
        greet(device(0, dz, 0))
        count += 1

    def copy(src, dst, send, recv, who):
        return pltpu.make_async_remote_copy(
            src_ref=src, dst_ref=dst, send_sem=send, recv_sem=recv, device_id=who, device_id_type=MESH
        )

    cosine = cos_in[...]
    sine = sin_in[...]

    def rotate(block):
        wide = block.astype(jnp.float32)
        return (wide * cosine + pltpu.roll(wide, HD // 2, 1) * sine).astype(jnp.bfloat16)

    for head in range(2):
        columns = slice(head * HD, (head + 1) * HD)
        kv_stage[head, 0] = rotate(k_in[:, columns])
        kv_stage[head, 1] = v_in[:, columns]
    kv[x, z, c] = kv_stage[x // 2]

    pl.semaphore_wait(barrier, count)

    def x_copy(dx):
        to = (x + dx) % NX
        return copy(kv_stage.at[to // 2], kv.at[x, z, c], a_s.at[dx], a_r.at[dx], device(dx, 0, 0))

    def x_arrival(dx):
        slot = kv.at[(x + NX - dx) % NX, z, c]
        return copy(slot, slot, a_s.at[dx], a_r.at[dx], sibling)

    def order(j):
        return j + j // 2 - 2 * (j // 3)

    def block_of(j, r):
        return kv.at[(x + NX - order(j)) % NX, (z + r) % NZ, c]

    def ring_copy(j, r, to_r, dz):
        block = block_of(j, r)
        return copy(block, block, z_s.at[j, to_r], z_r.at[j, to_r], device(0, dz, 0))

    def share_copy(j, r):
        block = block_of(j, r)
        return copy(block, block, sh_s.at[j, r], sh_r.at[j, r], sibling)

    def share_arrival(j, r):
        block = kv.at[(x + NX - order(j)) % NX, (z + r) % NZ, 1 - c]
        return copy(block, block, sh_s.at[j, r], sh_r.at[j, r], sibling)

    for dx in (1, 3, 2):
        x_copy(dx).start()
    ring_copy(0, 0, 7, 1).start()
    ring_copy(0, 0, 1, NZ - 1).start()
    share_copy(0, 0).start()

    for head in range(8):
        q_stage[head] = rotate(q_in[:, head * HD : (head + 1) * HD])
    qbuf[x, c] = q_stage[2 * x + c]

    def q_copy(dx, dc):
        head = 2 * ((x + dx) % NX) + (c + dc) % 2
        return copy(q_stage.at[head], qbuf.at[x, c], q_s.at[dx, dc], q_r.at[dx, dc], device(dx, 0, dc))

    def q_arrival(dx, dc):
        slot = qbuf.at[(x + NX - dx) % NX, (c + dc) % 2]
        return copy(slot, slot, q_s.at[dx, dc], q_r.at[dx, dc], sibling)

    partners = [(0, 1), (1, 0), (1, 1), (3, 0), (3, 1), (2, 0), (2, 1)]
    for dx, dc in partners:
        q_copy(dx, dc).start()

    wbuf[z, c] = w_in[...]

    def w_copy(r, to_r, dz):
        block = wbuf.at[(z + r) % NZ, c]
        return copy(block, block, w_s.at[to_r], w_r.at[to_r], device(0, dz, 0))

    def w_share(r):
        block = wbuf.at[(z + r) % NZ, c]
        return copy(block, block, wsh_s.at[r], wsh_r.at[r], sibling)

    def w_share_arrival(r):
        block = wbuf.at[(z + r) % NZ, 1 - c]
        return copy(block, block, wsh_s.at[r], wsh_r.at[r], sibling)

    ends = []
    end = len_ref[0]
    for number in range(6):
        ends.append(end)
        if number < 5:
            end = end + len_ref[number + 1]
    row_iota = lax.broadcasted_iota(jnp.int32, (2 * ROWS, HD), 0)

    def prepare(row, _):
        token = row * (16 * ROWS) + z * (2 * ROWS) + row_iota
        start = jnp.zeros((2 * ROWS, HD), jnp.int32)
        for end in ends:
            start = jnp.where(token >= end, end, start)
        start_ref[row] = start
        m_ref[row] = jnp.full((2 * ROWS, HD), LOW, jnp.float32)
        l_ref[row] = jnp.zeros((2 * ROWS, HD), jnp.float32)
        acc_ref[row] = jnp.zeros((2 * ROWS, HD), jnp.float32)
        return 0

    lax.fori_loop(0, NX, prepare, 0)

    for j, dx in ((1, 1), (2, 3), (3, 2)):
        x_arrival(dx).wait_recv()
        ring_copy(j, 0, 7, 1).start()
        ring_copy(j, 0, 1, NZ - 1).start()
        share_copy(j, 0).start()

    def twice(value):
        return jnp.concatenate([value, value], axis=1)

    def attend(j, r):
        share_arrival(j, r).wait_recv()
        xk = (x + NX - order(j)) % NX
        zk = (z + r) % NZ
        key_first = xk * (16 * ROWS) + zk * (2 * ROWS)

        def one_row(row, _):
            apart = 8 * (row - xk) + z - zk

            @pl.when((apart >= 0) & (apart <= 20))
            def _():
                q = qbuf[row].reshape(2 * ROWS, HD)
                k = kv[xk, zk, :, 0].reshape(2 * ROWS, HD)
                v = kv[xk, zk, :, 1].reshape(2 * ROWS, HD)
                raw = lax.dot_general(
                    q, k, (((1,), (1,)), ((), ())), preferred_element_type=jnp.float32
                )
                key = key_first + lax.broadcasted_iota(jnp.int32, (2 * ROWS, 2 * ROWS), 1)
                token = (
                    row * (16 * ROWS)
                    + z * (2 * ROWS)
                    + lax.broadcasted_iota(jnp.int32, (2 * ROWS, 2 * ROWS), 0)
                )
                visible = (key >= twice(start_ref[row])) & (key <= token)
                raw = jnp.where(visible, raw, MASKED)
                old = m_ref[row]
                new = jnp.maximum(old, jnp.max(raw, axis=1, keepdims=True))
                shrink = jnp.exp2((old - new) * FACTOR)
                weights = jnp.exp2((raw - twice(new)) * FACTOR)
                l_ref[row] = l_ref[row] * shrink + jnp.sum(weights, axis=1, keepdims=True)
                acc_ref[row] = acc_ref[row] * shrink + jnp.dot(
                    weights.astype(jnp.bfloat16), v, preferred_element_type=jnp.float32
                )
                m_ref[row] = new

            return 0

        lax.fori_loop(xk, NX, one_row, 0)

    def item(m):
        d = 1 + m // 8
        j = (m // 2) % 4
        s = m % 2
        return d, j, s, (1 - s) * (NZ - d) + s * d

    def arrive(m):
        d, j, s, r = item(m)
        block = block_of(j, r)
        copy(block, block, z_s.at[j, r], z_r.at[j, r], sibling).wait_recv()

        @pl.when((d < 3) | (c == s))
        def _():
            ring_copy(j, r, r - 1 + 2 * s, (1 + 6 * s)).start()

        share_copy(j, r).start()

    def first_items(m, _):
        arrive(m)
        attend(m, 0)
        return 0

    def middle_items(m, _):
        arrive(m)
        _, j, _, r = item(m - 4)
        attend(j, r)
        return 0

    def last_items(m, _):
        block = block_of(m, 4)
        copy(block, block, z_s.at[m, 4], z_r.at[m, 4], sibling).wait_recv()
        share_copy(m, 4).start()
        _, j, _, r = item(m + 20)
        attend(j, r)
        return 0

    def final_items(m, _):
        attend(m, 4)
        return 0

    for dx, dc in partners:
        q_arrival(dx, dc).wait_recv()
    lax.fori_loop(0, 4, first_items, 0)
    lax.fori_loop(4, 24, middle_items, 0)

    w_copy(0, 7, 1).start()
    w_copy(0, 1, NZ - 1).start()
    w_share(0).start()

    lax.fori_loop(0, 4, last_items, 0)
    lax.fori_loop(0, 4, final_items, 0)

    def finish(row, _):
        done = (acc_ref[row] / l_ref[row]).astype(jnp.bfloat16)
        own_att[0, row] = done[:ROWS]
        own_att[1, row] = done[ROWS:]
        return 0

    lax.fori_loop(0, NX, finish, 0)

    def g_copy(dx, dc):
        return copy(
            own_att.at[(c + dc) % 2], att.at[2 * x + c], g_s.at[dx, dc], g_r.at[dx, dc], device(dx, 0, dc)
        )

    def g_arrival(dx, dc):
        slot = att.at[2 * ((x + NX - dx) % NX) + (c + dc) % 2]
        return copy(slot, slot, g_s.at[dx, dc], g_r.at[dx, dc], sibling)

    for dx, dc in partners:
        g_copy(dx, dc).start()
    att[2 * x + c] = own_att[c]

    def w_step(n, _):
        d = 1 + n // 2
        s = n % 2
        r = (1 - s) * (NZ - d) + s * d
        block = wbuf.at[(z + r) % NZ, c]
        copy(block, block, w_s.at[r], w_r.at[r], sibling).wait_recv()

        @pl.when((d < 3) | (c == s))
        def _():
            w_copy(r, r - 1 + 2 * s, 1 + 6 * s).start()

        w_share(r).start()
        return 0

    lax.fori_loop(0, 6, w_step, 0)
    last_w = wbuf.at[(z + 4) % NZ, c]
    copy(last_w, last_w, w_s.at[4], w_r.at[4], sibling).wait_recv()
    w_share(4).start()

    for dx, dc in partners:
        g_arrival(dx, dc).wait_recv()

    def w_wait(r, _):
        w_share_arrival(r).wait_recv()
        return 0

    lax.fori_loop(0, NZ, w_wait, 0)

    def e_copy(row, nb):
        return copy(
            pbuf.at[row, nb], part.at[y, nb], e_s.at[row, nb], e_r.at[y, nb], (row * 16 + z * 2 + c, x)
        )

    def project(nb, _):
        left = jnp.concatenate([att[head].reshape(4 * ROWS, HD) for head in range(8)], axis=1)
        right = wbuf[pl.ds(2 * nb, 2)].reshape(2 * HD, 8 * HD)
        product = lax.dot_general(
            left, right, (((1,), (1,)), ((), ())), preferred_element_type=jnp.float32
        ).astype(jnp.bfloat16)
        for row in range(NX):
            pbuf[row, nb] = product[row * ROWS : (row + 1) * ROWS]
        for row in range(NX):
            mine = (x == row) & (y == x)

            @pl.when(mine)
            def _():
                part[y, nb] = pbuf[row, nb]

            @pl.when(jnp.logical_not(mine))
            def _():
                e_copy(row, nb).start()

        return 0

    lax.fori_loop(0, 4, project, 0)

    for nb in range(4):
        for source in range(NY):
            slot = part.at[source, nb]
            arrival = copy(slot, slot, e_s.at[source, nb], e_r.at[source, nb], sibling)

            @pl.when(jnp.logical_not((x == y) & (source == y)))
            def _():
                arrival.wait_recv()

        total = part[0, nb].astype(jnp.float32)
        for source in range(1, NY):
            total = total + part[source, nb].astype(jnp.float32)
        out_ref[:, nb * 256 : (nb + 1) * 256] = total.astype(jnp.bfloat16)

    for dx in (1, 3, 2):
        x_copy(dx).wait_send()
    for dx, dc in partners:
        q_copy(dx, dc).wait_send()
        g_copy(dx, dc).wait_send()

    def sent(n, _):
        j = n % 4
        r = n // 4
        share_copy(j, r).wait_send()
        return 0

    lax.fori_loop(0, 32, sent, 0)

    def ring_sent(n, _):
        j = n % 4
        r = 1 + n // 4
        block = block_of(j, r)
        copy(block, block, z_s.at[j, r], z_r.at[j, r], sibling).wait_send()
        return 0

    lax.fori_loop(0, 28, ring_sent, 0)

    def w_sent(r, _):
        w_share(r).wait_send()
        return 0

    lax.fori_loop(0, NZ, w_sent, 0)

    def w_ring_sent(r, _):
        block = wbuf.at[(z + r) % NZ, c]
        copy(block, block, w_s.at[r], w_r.at[r], sibling).wait_send()
        return 0

    lax.fori_loop(1, NZ, w_ring_sent, 0)
    for row in range(NX):
        mine = (x == row) & (y == x)

        @pl.when(jnp.logical_not(mine))
        def _():
            for nb in range(4):
                e_copy(row, nb).wait_send()


def shards(queries, keys, values, out_weight, doc_lengths):
    cosine, sine = rotary_tables(doc_lengths)
    vmem = pl.BlockSpec(memory_space=pltpu.VMEM)
    bf16, f32 = jnp.bfloat16, jnp.float32
    dma = pltpu.SemaphoreType.DMA
    return pl.pallas_call(
        kernel,
        out_shape=jax.ShapeDtypeStruct((ROWS, 1024), bf16),
        in_specs=[vmem] * 6 + [pl.BlockSpec(memory_space=pltpu.SMEM)],
        out_specs=vmem,
        scratch_shapes=[
            pltpu.VMEM((8, ROWS, HD), bf16),
            pltpu.VMEM((2, 2, ROWS, HD), bf16),
            pltpu.VMEM((NX, 2, ROWS, HD), bf16),
            pltpu.VMEM((NX, NZ, 2, 2, ROWS, HD), bf16),
            pltpu.VMEM((NX, 2 * ROWS, HD), jnp.int32),
            pltpu.VMEM((NX, 2 * ROWS, HD), f32),
            pltpu.VMEM((NX, 2 * ROWS, HD), f32),
            pltpu.VMEM((NX, 2 * ROWS, HD), f32),
            pltpu.VMEM((2, NX, ROWS, HD), bf16),
            pltpu.VMEM((8, NX, ROWS, HD), bf16),
            pltpu.VMEM((NZ, 2, 64, 1024), bf16),
            pltpu.VMEM((NX, 4, ROWS, 256), bf16),
            pltpu.VMEM((NY, 4, ROWS, 256), bf16),
            dma((4,)), dma((4,)),
            dma((4, 2)), dma((4, 2)),
            dma((4, 8)), dma((4, 8)),
            dma((4, 8)), dma((4, 8)),
            dma((4, 2)), dma((4, 2)),
            dma((8,)), dma((8,)),
            dma((8,)), dma((8,)),
            dma((4, 4)), dma((4, 4)),
        ],
        compiler_params=pltpu.CompilerParams(
            collective_id=0, has_side_effects=True, vmem_limit_bytes=48 << 20
        ),
    )(queries, keys, values, out_weight.T, cosine, sine, doc_lengths)


def solution(mesh):
    in_specs = (P("tok", "feat"), P("tok", "feat"), P("tok", "feat"), P("feat", "tok"), P())
    return jax.shard_map(
        shards, mesh=mesh, in_specs=in_specs, out_specs=P("tok", "feat"), check_vma=False
    )
```

```python
import functools

import jax
import jax.numpy as jnp
import numpy as np
from jax import lax
from jax.experimental import pallas as pl
from jax.experimental.pallas import tpu as pltpu
from jax.sharding import PartitionSpec as P

HD = 128
ROPE_BASE = 500000.0
LOW = -1e30
MASKED = -2e30
ROWS = 128
NX, NZ, NY = 4, 8, 4
FACTOR = float(HD**-0.5 * np.log2(np.e))
MESH = pl.DeviceIdType.MESH


def frequencies():
    half = HD // 2
    frequency = ROPE_BASE ** (-(np.arange(half, dtype=np.float64) * 2.0 / HD))
    return np.concatenate([frequency, frequency]).astype(np.float32).reshape(1, HD)


def kernel(
    q_hbm, k_hbm, v_hbm, w_hbm, freq_ref, len_ref, out_ref,
    q_in, k_in, v_in, in_sem, q_stage, kv_stage, qbuf, kv, start_ref, m_ref, l_ref, acc_ref, own_att, att, wbuf, pbuf, part,
    a_s, a_r, q_s, q_r, z_s, z_r, sh_s, sh_r, g_s, g_r, w_s, w_r, wsh_s, wsh_r, e_s, e_r,
):
    t = lax.axis_index("tok")
    y = lax.axis_index("feat")
    x = t // 16
    z = (t // 2) % NZ
    c = t % 2

    def device(dx, dz, dc):
        return (((x + dx) % NX) * 16 + ((z + dz) % NZ) * 2 + (c + dc) % 2, y)

    sibling = device(0, 0, 1)

    loads = [
        pltpu.make_async_copy(k_hbm, k_in, in_sem.at[0]),
        pltpu.make_async_copy(v_hbm, v_in, in_sem.at[1]),
        pltpu.make_async_copy(q_hbm, q_in, in_sem.at[2]),
        pltpu.make_async_copy(w_hbm, wbuf.at[z, c], in_sem.at[3]),
    ]
    for load in loads:
        load.start()

    barrier = pltpu.get_barrier_semaphore()
    count = 0

    def greet(who):
        pl.semaphore_signal(barrier, inc=1, device_id=who, device_id_type=MESH)

    for dx in range(NX):
        for dy in range(NY):
            if dx or dy:
                greet((((x + dx) % NX) * 16 + z * 2 + c, (y + dy) % NY))
                count += 1
        greet(device(dx, 0, 1))
        count += 1
    for dz in (1, NZ - 1):
        greet(device(0, dz, 0))
        count += 1

    def copy(src, dst, send, recv, who):
        return pltpu.make_async_remote_copy(
            src_ref=src, dst_ref=dst, send_sem=send, recv_sem=recv, device_id=who, device_id_type=MESH
        )

    ends = []
    end = len_ref[0]
    for number in range(5):
        ends.append(end)
        end = end + len_ref[number + 1]

    def first_token(token):
        start = jnp.zeros(token.shape, jnp.int32)
        for end in ends:
            start = jnp.where(token >= end, end, start)
        return start

    token = t * ROWS + lax.broadcasted_iota(jnp.int32, (ROWS, HD), 0)
    angles = (token - first_token(token)).astype(jnp.float32) * freq_ref[...]
    cosine = jnp.cos(angles)
    sine = jnp.sin(angles)
    sine = jnp.where(lax.broadcasted_iota(jnp.int32, (ROWS, HD), 1) < HD // 2, -sine, sine)

    def rotate(block):
        wide = block.astype(jnp.float32)
        return wide * cosine + pltpu.roll(wide, HD // 2, 1) * sine

    loads[0].wait()
    loads[1].wait()
    for head in range(2):
        columns = slice(head * HD, (head + 1) * HD)
        kv_stage[head, 0] = rotate(k_in[:, columns]).T.astype(jnp.bfloat16)
        kv_stage[head, 1] = v_in[:, columns]
    kv[x, z, c] = kv_stage[x // 2]

    pl.semaphore_wait(barrier, count)

    def x_copy(dx):
        to = (x + dx) % NX
        return copy(kv_stage.at[to // 2], kv.at[x, z, c], a_s.at[dx], a_r.at[dx], device(dx, 0, 0))

    def x_arrival(dx):
        slot = kv.at[(x + NX - dx) % NX, z, c]
        return copy(slot, slot, a_s.at[dx], a_r.at[dx], sibling)

    def order(j):
        return j + j // 2 - 2 * (j // 3)

    def block_of(j, r):
        return kv.at[(x + NX - order(j)) % NX, (z + r) % NZ, c]

    def ring_copy(j, r, to_r, dz):
        block = block_of(j, r)
        return copy(block, block, z_s.at[j, to_r], z_r.at[j, to_r], device(0, dz, 0))

    def share_copy(j, r):
        block = block_of(j, r)
        return copy(block, block, sh_s.at[j, r], sh_r.at[j, r], sibling)

    def share_arrival(j, r):
        block = kv.at[(x + NX - order(j)) % NX, (z + r) % NZ, 1 - c]
        return copy(block, block, sh_s.at[j, r], sh_r.at[j, r], sibling)

    def w_copy(r, to_r, dz):
        block = wbuf.at[(z + r) % NZ, c]
        return copy(block, block, w_s.at[to_r], w_r.at[to_r], device(0, dz, 0))

    def w_share(r):
        block = wbuf.at[(z + r) % NZ, c]
        return copy(block, block, wsh_s.at[r], wsh_r.at[r], sibling)

    def w_share_arrival(r):
        block = wbuf.at[(z + r) % NZ, 1 - c]
        return copy(block, block, wsh_s.at[r], wsh_r.at[r], sibling)

    for dx in (1, 3, 2):
        x_copy(dx).start()
    ring_copy(0, 0, 7, 1).start()
    ring_copy(0, 0, 1, NZ - 1).start()
    share_copy(0, 0).start()
    loads[3].wait()
    w_copy(0, 7, 1).start()
    w_copy(0, 1, NZ - 1).start()
    w_share(0).start()
    loads[2].wait()

    for head in range(8):
        q_stage[head] = rotate(q_in[:, head * HD : (head + 1) * HD]).astype(jnp.bfloat16)
    qbuf[x, c] = q_stage[2 * x + c]

    def q_copy(dx, dc):
        head = 2 * ((x + dx) % NX) + (c + dc) % 2
        return copy(q_stage.at[head], qbuf.at[x, c], q_s.at[dx, dc], q_r.at[dx, dc], device(dx, 0, dc))

    def q_arrival(dx, dc):
        slot = qbuf.at[(x + NX - dx) % NX, (c + dc) % 2]
        return copy(slot, slot, q_s.at[dx, dc], q_r.at[dx, dc], sibling)

    partners = [(0, 1), (1, 0), (1, 1), (3, 0), (3, 1), (2, 0), (2, 1)]
    for dx, dc in partners:
        q_copy(dx, dc).start()

    row_iota = lax.broadcasted_iota(jnp.int32, (2 * ROWS, HD), 0)

    def prepare(row, _):
        token = row * (16 * ROWS) + z * (2 * ROWS) + row_iota
        start_ref[row] = first_token(token)
        m_ref[row] = jnp.full((2 * ROWS, HD), LOW, jnp.float32)
        l_ref[row] = jnp.zeros((2 * ROWS, HD), jnp.float32)
        acc_ref[row] = jnp.zeros((2 * ROWS, HD), jnp.float32)
        return 0

    lax.fori_loop(0, NX, prepare, 0)

    for j, dx in ((1, 1), (2, 3), (3, 2)):
        x_arrival(dx).wait_recv()
        ring_copy(j, 0, 7, 1).start()
        ring_copy(j, 0, 1, NZ - 1).start()
        share_copy(j, 0).start()

    def attend_rows(rows, r):
        zk = (z + r) % NZ
        lane = lax.broadcasted_iota(jnp.int32, (2 * ROWS, HD), 1)
        keys = [
            jnp.concatenate([kv[xk, zk, 0, 0], kv[xk, zk, 1, 0]], axis=1)
            for xk in range(max(rows) + 1)
        ]
        scores = []
        for row in rows:
            q = qbuf[row].reshape(2 * ROWS, HD)
            scores.append(
                [jnp.dot(q, keys[xk], preferred_element_type=jnp.float32) for xk in range(row + 1)]
            )
        for row, raws in zip(rows, scores):
            start = start_ref[row]
            token = row * (16 * ROWS) + z * (2 * ROWS) + row_iota
            pieces = []
            for xk, raw in enumerate(raws):
                for side in range(2):
                    key = xk * (16 * ROWS) + zk * (2 * ROWS) + side * HD + lane
                    visible = key >= start
                    if xk == row:
                        visible = visible & (key <= token)
                    piece = raw[:, side * HD : (side + 1) * HD]
                    pieces.append(jnp.where(visible, piece, MASKED))
            old = m_ref[row]
            new = jnp.maximum(
                old, jnp.max(functools.reduce(jnp.maximum, pieces), axis=1, keepdims=True)
            )
            shrink = jnp.exp2((old - new) * FACTOR)
            weights = [jnp.exp2((piece - new) * FACTOR) for piece in pieces]
            m_ref[row] = new
            l_ref[row] = l_ref[row] * shrink + functools.reduce(jnp.add, weights)
            v = kv[0 : row + 1, zk, :, 1].reshape((row + 1) * 2 * ROWS, HD)
            acc_ref[row] = acc_ref[row] * shrink + jnp.dot(
                jnp.concatenate([weight.astype(jnp.bfloat16) for weight in weights], axis=1),
                v,
                preferred_element_type=jnp.float32,
            )

    def attend_unit(unit, _):
        group = unit // 2
        odd = group % 2
        d = (group + 1) // 2
        r = odd * (NZ - d) + (1 - odd) * d

        @pl.when(unit % 2 == 0)
        def _():
            for j in range(4):
                share_arrival(j, r).wait_recv()
            attend_rows((0, 3), r)

        @pl.when(unit % 2 == 1)
        def _():
            attend_rows((1, 2), r)

        return 0

    def item(m):
        d = 1 + m // 8
        j = (m // 2) % 4
        s = m % 2
        return d, j, s, (1 - s) * (NZ - d) + s * d

    def arrive(m):
        d, j, s, r = item(m)
        block = block_of(j, r)
        copy(block, block, z_s.at[j, r], z_r.at[j, r], sibling).wait_recv()

        @pl.when((d < 3) | (c == s))
        def _():
            ring_copy(j, r, r - 1 + 2 * s, (1 + 6 * s)).start()

        share_copy(j, r).start()

    def arrive_pair(p):
        arrive(2 * p)
        arrive(2 * p + 1)

    def hop(p, _):
        arrive_pair(p)
        return 0

    def w_step(n):
        d = 1 + n // 2
        s = n % 2
        r = (1 - s) * (NZ - d) + s * d
        block = wbuf.at[(z + r) % NZ, c]
        copy(block, block, w_s.at[r], w_r.at[r], sibling).wait_recv()

        @pl.when((d < 3) | (c == s))
        def _():
            w_copy(r, r - 1 + 2 * s, 1 + 6 * s).start()

        w_share(r).start()

    lax.fori_loop(0, 4, hop, 0)
    for dx, dc in partners:
        q_arrival(dx, dc).wait_recv()
    def first_unit(step):
        return step + (jnp.minimum(step, 3) + 1) // 2

    def ring_step(step, _):
        @pl.when(step < 8)
        def _():
            arrive_pair(step + 4)

        @pl.when(step == 8)
        def _():
            w_step(0)
            w_step(1)

        @pl.when((step >= 8) & (step < 12))
        def _():
            block = block_of(step - 8, 4)
            copy(block, block, z_s.at[step - 8, 4], z_r.at[step - 8, 4], sibling).wait_recv()
            share_copy(step - 8, 4).start()

        @pl.when(step == 12)
        def _():
            w_step(2)
            w_step(3)

        lax.fori_loop(first_unit(step), first_unit(step + 1), attend_unit, 0)
        return 0

    lax.fori_loop(0, 14, ring_step, 0)

    def finish(row, _):
        total = jnp.sum(l_ref[row], axis=1, keepdims=True)
        done = (acc_ref[row] / total).astype(jnp.bfloat16)
        own_att[0, row] = done[:ROWS]
        own_att[1, row] = done[ROWS:]
        return 0

    lax.fori_loop(0, NX, finish, 0)

    def g_copy(dx, dc):
        return copy(
            own_att.at[(c + dc) % 2], att.at[2 * x + c], g_s.at[dx, dc], g_r.at[dx, dc], device(dx, 0, dc)
        )

    def g_arrival(dx, dc):
        slot = att.at[2 * ((x + NX - dx) % NX) + (c + dc) % 2]
        return copy(slot, slot, g_s.at[dx, dc], g_r.at[dx, dc], sibling)

    for dx, dc in partners:
        g_copy(dx, dc).start()
    att[2 * x + c] = own_att[c]

    w_step(4)
    w_step(5)
    last_w = wbuf.at[(z + 4) % NZ, c]
    copy(last_w, last_w, w_s.at[4], w_r.at[4], sibling).wait_recv()
    w_share(4).start()

    for dx, dc in partners:
        g_arrival(dx, dc).wait_recv()

    def w_wait(r, _):
        w_share_arrival(r).wait_recv()
        return 0

    lax.fori_loop(0, NZ, w_wait, 0)

    def e_copy(row, nb):
        return copy(
            pbuf.at[row, nb], part.at[y, nb], e_s.at[row, nb], e_r.at[y, nb], (row * 16 + z * 2 + c, x)
        )

    def project(nb, _):
        left = jnp.concatenate([att[head].reshape(4 * ROWS, HD) for head in range(8)], axis=1)
        right = wbuf[pl.ds(2 * nb, 2)].reshape(2 * HD, 8 * HD)
        product = lax.dot_general(
            left, right, (((1,), (1,)), ((), ())), preferred_element_type=jnp.float32
        ).astype(jnp.bfloat16)
        for row in range(NX):
            pbuf[row, nb] = product[row * ROWS : (row + 1) * ROWS]
        for row in range(NX):
            mine = (x == row) & (y == x)

            @pl.when(mine)
            def _():
                part[y, nb] = pbuf[row, nb]

            @pl.when(jnp.logical_not(mine))
            def _():
                e_copy(row, nb).start()

        return 0

    lax.fori_loop(0, 4, project, 0)

    for nb in range(4):
        for source in range(NY):
            slot = part.at[source, nb]
            arrival = copy(slot, slot, e_s.at[source, nb], e_r.at[source, nb], sibling)

            @pl.when(jnp.logical_not((x == y) & (source == y)))
            def _():
                arrival.wait_recv()

        total = part[0, nb].astype(jnp.float32)
        for source in range(1, NY):
            total = total + part[source, nb].astype(jnp.float32)
        out_ref[:, nb * 256 : (nb + 1) * 256] = total.astype(jnp.bfloat16)

    for dx in (1, 3, 2):
        x_copy(dx).wait_send()
    for dx, dc in partners:
        q_copy(dx, dc).wait_send()
        g_copy(dx, dc).wait_send()

    def sent(n, _):
        j = n % 4
        r = n // 4
        share_copy(j, r).wait_send()
        return 0

    lax.fori_loop(0, 32, sent, 0)

    def ring_sent(n, _):
        j = n % 4
        r = 1 + n // 4
        block = block_of(j, r)
        copy(block, block, z_s.at[j, r], z_r.at[j, r], sibling).wait_send()
        return 0

    lax.fori_loop(0, 28, ring_sent, 0)

    def w_sent(r, _):
        w_share(r).wait_send()
        return 0

    lax.fori_loop(0, NZ, w_sent, 0)

    def w_ring_sent(r, _):
        block = wbuf.at[(z + r) % NZ, c]
        copy(block, block, w_s.at[r], w_r.at[r], sibling).wait_send()
        return 0

    lax.fori_loop(1, NZ, w_ring_sent, 0)
    for row in range(NX):
        mine = (x == row) & (y == x)

        @pl.when(jnp.logical_not(mine))
        def _():
            for nb in range(4):
                e_copy(row, nb).wait_send()


def shards(queries, keys, values, out_weight, doc_lengths):
    vmem = pl.BlockSpec(memory_space=pltpu.VMEM)
    hbm = pl.BlockSpec(memory_space=pltpu.HBM)
    bf16, f32 = jnp.bfloat16, jnp.float32
    dma = pltpu.SemaphoreType.DMA
    return pl.pallas_call(
        kernel,
        out_shape=jax.ShapeDtypeStruct((ROWS, 1024), bf16),
        in_specs=[hbm] * 4 + [vmem, pl.BlockSpec(memory_space=pltpu.SMEM)],
        out_specs=vmem,
        scratch_shapes=[
            pltpu.VMEM((ROWS, 1024), bf16),
            pltpu.VMEM((ROWS, 256), bf16),
            pltpu.VMEM((ROWS, 256), bf16),
            dma((4,)),
            pltpu.VMEM((8, ROWS, HD), bf16),
            pltpu.VMEM((2, 2, ROWS, HD), bf16),
            pltpu.VMEM((NX, 2, ROWS, HD), bf16),
            pltpu.VMEM((NX, NZ, 2, 2, ROWS, HD), bf16),
            pltpu.VMEM((NX, 2 * ROWS, HD), jnp.int32),
            pltpu.VMEM((NX, 2 * ROWS, HD), f32),
            pltpu.VMEM((NX, 2 * ROWS, HD), f32),
            pltpu.VMEM((NX, 2 * ROWS, HD), f32),
            pltpu.VMEM((2, NX, ROWS, HD), bf16),
            pltpu.VMEM((8, NX, ROWS, HD), bf16),
            pltpu.VMEM((NZ, 2, 64, 1024), bf16),
            pltpu.VMEM((NX, 4, ROWS, 256), bf16),
            pltpu.VMEM((NY, 4, ROWS, 256), bf16),
            dma((4,)), dma((4,)),
            dma((4, 2)), dma((4, 2)),
            dma((4, 8)), dma((4, 8)),
            dma((4, 8)), dma((4, 8)),
            dma((4, 2)), dma((4, 2)),
            dma((8,)), dma((8,)),
            dma((8,)), dma((8,)),
            dma((4, 4)), dma((4, 4)),
        ],
        compiler_params=pltpu.CompilerParams(
            collective_id=0, has_side_effects=True, vmem_limit_bytes=56 << 20
        ),
    )(queries, keys, values, out_weight.T, jnp.asarray(frequencies()), doc_lengths)


def solution(mesh):
    in_specs = (P("tok", "feat"), P("tok", "feat"), P("tok", "feat"), P("feat", "tok"), P())
    return jax.shard_map(
        shards, mesh=mesh, in_specs=in_specs, out_specs=P("tok", "feat"), check_vma=False
    )
```

```python
import functools

import jax
import jax.numpy as jnp
import numpy as np
from jax import lax
from jax.experimental import pallas as pl
from jax.experimental.pallas import tpu as pltpu
from jax.sharding import PartitionSpec as P

HD = 128
ROPE_BASE = 500000.0
LOW = -1e30
MASKED = -2e30
ROWS = 128
NX, NZ, NY = 4, 8, 4
FACTOR = float(HD**-0.5 * np.log2(np.e))
MESH = pl.DeviceIdType.MESH


def frequencies():
    half = HD // 2
    frequency = ROPE_BASE ** (-(np.arange(half, dtype=np.float64) * 2.0 / HD))
    return np.concatenate([frequency, frequency]).astype(np.float32).reshape(1, HD)


def kernel(
    q_hbm, k_hbm, v_hbm, w_hbm, freq_hbm, len_hbm, out_ref,
    freq_ref, len_ref, q_in, k_in, v_in, in_sem, q_stage, kv_stage, qbuf, kv, start_ref, m_ref, l_ref, acc_ref, own_att, att, wbuf, pbuf, part,
    a_s, a_r, q_s, q_r, z_s, z_r, sh_s, sh_r, g_s, g_r, w_s, w_r, wsh_s, wsh_r, e_s, e_r,
):
    t = lax.axis_index("tok")
    y = lax.axis_index("feat")
    x = t // 16
    z = (t // 2) % NZ
    c = t % 2

    def device(dx, dz, dc):
        return (((x + dx) % NX) * 16 + ((z + dz) % NZ) * 2 + (c + dc) % 2, y)

    sibling = device(0, 0, 1)

    barrier = pltpu.get_barrier_semaphore()
    count = 0

    def greet(who):
        pl.semaphore_signal(barrier, inc=1, device_id=who, device_id_type=MESH)

    for dx in range(NX):
        for dy in range(NY):
            if dx or dy:
                greet((((x + dx) % NX) * 16 + z * 2 + c, (y + dy) % NY))
                count += 1
        greet(device(dx, 0, 1))
        count += 1
    for dz in (1, NZ - 1):
        greet(device(0, dz, 0))
        count += 1

    loads = [
        pltpu.make_async_copy(k_hbm, k_in, in_sem.at[0]),
        pltpu.make_async_copy(v_hbm, v_in, in_sem.at[1]),
        pltpu.make_async_copy(q_hbm, q_in, in_sem.at[2]),
        pltpu.make_async_copy(w_hbm, wbuf.at[z, c], in_sem.at[3]),
        pltpu.make_async_copy(freq_hbm, freq_ref, in_sem.at[4]),
        pltpu.make_async_copy(len_hbm, len_ref, in_sem.at[5]),
    ]
    for load in loads:
        load.start()

    def copy(src, dst, send, recv, who):
        return pltpu.make_async_remote_copy(
            src_ref=src, dst_ref=dst, send_sem=send, recv_sem=recv, device_id=who, device_id_type=MESH
        )

    loads[4].wait()
    loads[5].wait()
    ends = []
    end = len_ref[0]
    for number in range(5):
        ends.append(end)
        end = end + len_ref[number + 1]

    def first_token(token):
        start = jnp.zeros(token.shape, jnp.int32)
        for end in ends:
            start = jnp.where(token >= end, end, start)
        return start

    token = t * ROWS + lax.broadcasted_iota(jnp.int32, (ROWS, HD), 0)
    angles = (token - first_token(token)).astype(jnp.float32) * freq_ref[...]
    cosine = jnp.cos(angles)
    sine = jnp.sin(angles)
    sine = jnp.where(lax.broadcasted_iota(jnp.int32, (ROWS, HD), 1) < HD // 2, -sine, sine)

    def rotate(block):
        wide = block.astype(jnp.float32)
        return wide * cosine + pltpu.roll(wide, HD // 2, 1) * sine

    loads[0].wait()
    loads[1].wait()
    for head in range(2):
        columns = slice(head * HD, (head + 1) * HD)
        kv_stage[head, 0] = rotate(k_in[:, columns]).T.astype(jnp.bfloat16)
        kv_stage[head, 1] = v_in[:, columns]
    kv[x, z, c] = kv_stage[x // 2]

    pl.semaphore_wait(barrier, count)

    def x_copy(dx):
        to = (x + dx) % NX
        return copy(kv_stage.at[to // 2], kv.at[x, z, c], a_s.at[dx], a_r.at[dx], device(dx, 0, 0))

    def x_arrival(dx):
        slot = kv.at[(x + NX - dx) % NX, z, c]
        return copy(slot, slot, a_s.at[dx], a_r.at[dx], sibling)

    def order(j):
        return j + j // 2 - 2 * (j // 3)

    def block_of(j, r):
        return kv.at[(x + NX - order(j)) % NX, (z + r) % NZ, c]

    def ring_copy(j, r, to_r, dz):
        block = block_of(j, r)
        return copy(block, block, z_s.at[j, to_r], z_r.at[j, to_r], device(0, dz, 0))

    def share_copy(j, r):
        block = block_of(j, r)
        return copy(block, block, sh_s.at[j, r], sh_r.at[j, r], sibling)

    def share_arrival(j, r):
        block = kv.at[(x + NX - order(j)) % NX, (z + r) % NZ, 1 - c]
        return copy(block, block, sh_s.at[j, r], sh_r.at[j, r], sibling)

    def w_copy(r, to_r, dz):
        block = wbuf.at[(z + r) % NZ, c]
        return copy(block, block, w_s.at[to_r], w_r.at[to_r], device(0, dz, 0))

    def w_share(r):
        block = wbuf.at[(z + r) % NZ, c]
        return copy(block, block, wsh_s.at[r], wsh_r.at[r], sibling)

    def w_share_arrival(r):
        block = wbuf.at[(z + r) % NZ, 1 - c]
        return copy(block, block, wsh_s.at[r], wsh_r.at[r], sibling)

    for dx in (1, 3, 2):
        x_copy(dx).start()
    ring_copy(0, 0, 7, 1).start()
    ring_copy(0, 0, 1, NZ - 1).start()
    share_copy(0, 0).start()
    loads[3].wait()
    w_copy(0, 7, 1).start()
    w_copy(0, 1, NZ - 1).start()
    w_share(0).start()
    loads[2].wait()

    for head in range(8):
        q_stage[head] = rotate(q_in[:, head * HD : (head + 1) * HD]).astype(jnp.bfloat16)
    qbuf[x, c] = q_stage[2 * x + c]

    def q_copy(dx, dc):
        head = 2 * ((x + dx) % NX) + (c + dc) % 2
        return copy(q_stage.at[head], qbuf.at[x, c], q_s.at[dx, dc], q_r.at[dx, dc], device(dx, 0, dc))

    def q_arrival(dx, dc):
        slot = qbuf.at[(x + NX - dx) % NX, (c + dc) % 2]
        return copy(slot, slot, q_s.at[dx, dc], q_r.at[dx, dc], sibling)

    partners = [(0, 1), (1, 0), (1, 1), (3, 0), (3, 1), (2, 0), (2, 1)]
    for dx, dc in partners:
        q_copy(dx, dc).start()

    row_iota = lax.broadcasted_iota(jnp.int32, (2 * ROWS, HD), 0)

    def prepare(row, _):
        token = row * (16 * ROWS) + z * (2 * ROWS) + row_iota
        start_ref[row] = first_token(token)
        m_ref[row] = jnp.full((2 * ROWS, HD), LOW, jnp.float32)
        l_ref[row] = jnp.zeros((2 * ROWS, HD), jnp.float32)
        acc_ref[row] = jnp.zeros((2 * ROWS, HD), jnp.float32)
        return 0

    lax.fori_loop(0, NX, prepare, 0)

    for j, dx in ((1, 1), (2, 3), (3, 2)):
        x_arrival(dx).wait_recv()
        ring_copy(j, 0, 7, 1).start()
        ring_copy(j, 0, 1, NZ - 1).start()
        share_copy(j, 0).start()

    def attend_rows(rows, r):
        zk = (z + r) % NZ
        lane = lax.broadcasted_iota(jnp.int32, (2 * ROWS, HD), 1)
        keys = [
            jnp.concatenate([kv[xk, zk, 0, 0], kv[xk, zk, 1, 0]], axis=1)
            for xk in range(max(rows) + 1)
        ]
        scores = []
        for row in rows:
            q = qbuf[row].reshape(2 * ROWS, HD)
            scores.append(
                [jnp.dot(q, keys[xk], preferred_element_type=jnp.float32) for xk in range(row + 1)]
            )
        for row, raws in zip(rows, scores):
            start = start_ref[row]
            token = row * (16 * ROWS) + z * (2 * ROWS) + row_iota
            pieces = []
            for xk, raw in enumerate(raws):
                for side in range(2):
                    key = xk * (16 * ROWS) + zk * (2 * ROWS) + side * HD + lane
                    visible = key >= start
                    if xk == row:
                        visible = visible & (key <= token)
                    piece = raw[:, side * HD : (side + 1) * HD]
                    pieces.append(jnp.where(visible, piece, MASKED))
            old = m_ref[row]
            new = jnp.maximum(
                old, jnp.max(functools.reduce(jnp.maximum, pieces), axis=1, keepdims=True)
            )
            shrink = jnp.exp2((old - new) * FACTOR)
            weights = [jnp.exp2((piece - new) * FACTOR) for piece in pieces]
            m_ref[row] = new
            l_ref[row] = l_ref[row] * shrink + functools.reduce(jnp.add, weights)
            v = kv[0 : row + 1, zk, :, 1].reshape((row + 1) * 2 * ROWS, HD)
            acc_ref[row] = acc_ref[row] * shrink + jnp.dot(
                jnp.concatenate([weight.astype(jnp.bfloat16) for weight in weights], axis=1),
                v,
                preferred_element_type=jnp.float32,
            )

    def attend_unit(unit, _):
        group = unit // 2
        odd = group % 2
        d = (group + 1) // 2
        r = odd * (NZ - d) + (1 - odd) * d

        @pl.when(unit % 2 == 0)
        def _():
            for j in range(4):
                share_arrival(j, r).wait_recv()
            attend_rows((0, 3), r)

        @pl.when(unit % 2 == 1)
        def _():
            attend_rows((1, 2), r)

        return 0

    def item(m):
        d = 1 + m // 8
        j = (m // 2) % 4
        s = m % 2
        return d, j, s, (1 - s) * (NZ - d) + s * d

    def arrive(m):
        d, j, s, r = item(m)
        block = block_of(j, r)
        copy(block, block, z_s.at[j, r], z_r.at[j, r], sibling).wait_recv()

        @pl.when((d < 3) | (c == s))
        def _():
            ring_copy(j, r, r - 1 + 2 * s, (1 + 6 * s)).start()

        share_copy(j, r).start()

    def arrive_pair(p):
        arrive(2 * p)
        arrive(2 * p + 1)

    def hop(p, _):
        arrive_pair(p)
        return 0

    def w_step(n):
        d = 1 + n // 2
        s = n % 2
        r = (1 - s) * (NZ - d) + s * d
        block = wbuf.at[(z + r) % NZ, c]
        copy(block, block, w_s.at[r], w_r.at[r], sibling).wait_recv()

        @pl.when((d < 3) | (c == s))
        def _():
            w_copy(r, r - 1 + 2 * s, 1 + 6 * s).start()

        w_share(r).start()

    lax.fori_loop(0, 4, hop, 0)
    for dx, dc in partners:
        q_arrival(dx, dc).wait_recv()
    def first_unit(step):
        return step + (jnp.minimum(step, 3) + 1) // 2

    def ring_step(step, _):
        @pl.when(step < 8)
        def _():
            arrive_pair(step + 4)

        @pl.when(step == 8)
        def _():
            w_step(0)
            w_step(1)

        @pl.when((step >= 8) & (step < 12))
        def _():
            block = block_of(step - 8, 4)
            copy(block, block, z_s.at[step - 8, 4], z_r.at[step - 8, 4], sibling).wait_recv()
            share_copy(step - 8, 4).start()

        @pl.when(step == 12)
        def _():
            w_step(2)
            w_step(3)

        lax.fori_loop(first_unit(step), first_unit(step + 1), attend_unit, 0)
        return 0

    lax.fori_loop(0, 14, ring_step, 0)

    def finish(row, _):
        total = jnp.sum(l_ref[row], axis=1, keepdims=True)
        done = (acc_ref[row] / total).astype(jnp.bfloat16)
        own_att[0, row] = done[:ROWS]
        own_att[1, row] = done[ROWS:]
        return 0

    lax.fori_loop(0, NX, finish, 0)

    def g_copy(dx, dc):
        return copy(
            own_att.at[(c + dc) % 2], att.at[2 * x + c], g_s.at[dx, dc], g_r.at[dx, dc], device(dx, 0, dc)
        )

    def g_arrival(dx, dc):
        slot = att.at[2 * ((x + NX - dx) % NX) + (c + dc) % 2]
        return copy(slot, slot, g_s.at[dx, dc], g_r.at[dx, dc], sibling)

    for dx, dc in partners:
        g_copy(dx, dc).start()
    att[2 * x + c] = own_att[c]

    w_step(4)
    w_step(5)
    last_w = wbuf.at[(z + 4) % NZ, c]
    copy(last_w, last_w, w_s.at[4], w_r.at[4], sibling).wait_recv()
    w_share(4).start()

    for dx, dc in partners:
        g_arrival(dx, dc).wait_recv()

    def w_wait(r, _):
        w_share_arrival(r).wait_recv()
        return 0

    lax.fori_loop(0, NZ, w_wait, 0)

    def e_copy(row, nb):
        return copy(
            pbuf.at[row, nb], part.at[y, nb], e_s.at[row, nb], e_r.at[y, nb], (row * 16 + z * 2 + c, x)
        )

    def project(nb, _):
        left = jnp.concatenate([att[head].reshape(4 * ROWS, HD) for head in range(8)], axis=1)
        right = wbuf[pl.ds(2 * nb, 2)].reshape(2 * HD, 8 * HD)
        product = lax.dot_general(
            left, right, (((1,), (1,)), ((), ())), preferred_element_type=jnp.float32
        ).astype(jnp.bfloat16)
        for row in range(NX):
            pbuf[row, nb] = product[row * ROWS : (row + 1) * ROWS]
        for row in range(NX):
            mine = (x == row) & (y == x)

            @pl.when(mine)
            def _():
                part[y, nb] = pbuf[row, nb]

            @pl.when(jnp.logical_not(mine))
            def _():
                e_copy(row, nb).start()

        return 0

    lax.fori_loop(0, 4, project, 0)

    for nb in range(4):
        for source in range(NY):
            slot = part.at[source, nb]
            arrival = copy(slot, slot, e_s.at[source, nb], e_r.at[source, nb], sibling)

            @pl.when(jnp.logical_not((x == y) & (source == y)))
            def _():
                arrival.wait_recv()

        total = part[0, nb].astype(jnp.float32)
        for source in range(1, NY):
            total = total + part[source, nb].astype(jnp.float32)
        out_ref[:, nb * 256 : (nb + 1) * 256] = total.astype(jnp.bfloat16)

    for dx in (1, 3, 2):
        x_copy(dx).wait_send()
    for dx, dc in partners:
        q_copy(dx, dc).wait_send()
        g_copy(dx, dc).wait_send()

    def sent(n, _):
        j = n % 4
        r = n // 4
        share_copy(j, r).wait_send()
        return 0

    lax.fori_loop(0, 32, sent, 0)

    def ring_sent(n, _):
        j = n % 4
        r = 1 + n // 4
        block = block_of(j, r)
        copy(block, block, z_s.at[j, r], z_r.at[j, r], sibling).wait_send()
        return 0

    lax.fori_loop(0, 28, ring_sent, 0)

    def w_sent(r, _):
        w_share(r).wait_send()
        return 0

    lax.fori_loop(0, NZ, w_sent, 0)

    def w_ring_sent(r, _):
        block = wbuf.at[(z + r) % NZ, c]
        copy(block, block, w_s.at[r], w_r.at[r], sibling).wait_send()
        return 0

    lax.fori_loop(1, NZ, w_ring_sent, 0)
    for row in range(NX):
        mine = (x == row) & (y == x)

        @pl.when(jnp.logical_not(mine))
        def _():
            for nb in range(4):
                e_copy(row, nb).wait_send()


def shards(queries, keys, values, out_weight, doc_lengths):
    vmem = pl.BlockSpec(memory_space=pltpu.VMEM)
    hbm = pl.BlockSpec(memory_space=pltpu.HBM)
    bf16, f32 = jnp.bfloat16, jnp.float32
    dma = pltpu.SemaphoreType.DMA
    operands = (queries, keys, values, out_weight.T, jnp.asarray(frequencies()), doc_lengths)
    return pl.pallas_call(
        kernel,
        out_shape=jax.ShapeDtypeStruct((ROWS, 1024), bf16),
        in_specs=[hbm] * 6,
        out_specs=vmem,
        scratch_shapes=[
            pltpu.VMEM((1, HD), f32),
            pltpu.SMEM((6,), jnp.int32),
            pltpu.VMEM((ROWS, 1024), bf16),
            pltpu.VMEM((ROWS, 256), bf16),
            pltpu.VMEM((ROWS, 256), bf16),
            dma((6,)),
            pltpu.VMEM((8, ROWS, HD), bf16),
            pltpu.VMEM((2, 2, ROWS, HD), bf16),
            pltpu.VMEM((NX, 2, ROWS, HD), bf16),
            pltpu.VMEM((NX, NZ, 2, 2, ROWS, HD), bf16),
            pltpu.VMEM((NX, 2 * ROWS, HD), jnp.int32),
            pltpu.VMEM((NX, 2 * ROWS, HD), f32),
            pltpu.VMEM((NX, 2 * ROWS, HD), f32),
            pltpu.VMEM((NX, 2 * ROWS, HD), f32),
            pltpu.VMEM((2, NX, ROWS, HD), bf16),
            pltpu.VMEM((8, NX, ROWS, HD), bf16),
            pltpu.VMEM((NZ, 2, 64, 1024), bf16),
            pltpu.VMEM((NX, 4, ROWS, 256), bf16),
            pltpu.VMEM((NY, 4, ROWS, 256), bf16),
            dma((4,)), dma((4,)),
            dma((4, 2)), dma((4, 2)),
            dma((4, 8)), dma((4, 8)),
            dma((4, 8)), dma((4, 8)),
            dma((4, 2)), dma((4, 2)),
            dma((8,)), dma((8,)),
            dma((8,)), dma((8,)),
            dma((4, 4)), dma((4, 4)),
        ],
        compiler_params=pltpu.CompilerParams(
            collective_id=0, has_side_effects=True, vmem_limit_bytes=48 << 20
        ),
    )(*(pltpu.with_memory_space_constraint(array, pltpu.HBM) for array in operands))


def solution(mesh):
    in_specs = (P("tok", "feat"), P("tok", "feat"), P("tok", "feat"), P("feat", "tok"), P())
    return jax.shard_map(
        shards, mesh=mesh, in_specs=in_specs, out_specs=P("tok", "feat"), check_vma=False
    )
```

```python
import functools

import jax
import jax.numpy as jnp
import numpy as np
from jax import lax
from jax.experimental import pallas as pl
from jax.experimental.pallas import tpu as pltpu
from jax.sharding import PartitionSpec as P

HD = 128
ROPE_BASE = 500000.0
LOW = -1e30
MASKED = -2e30
ROWS = 128
NX, NZ, NY = 4, 8, 4
FACTOR = float(HD**-0.5 * np.log2(np.e))
MESH = pl.DeviceIdType.MESH


def frequencies():
    half = HD // 2
    frequency = ROPE_BASE ** (-(np.arange(half, dtype=np.float64) * 2.0 / HD))
    return np.concatenate([frequency, frequency]).astype(np.float32).reshape(1, HD)


def kernel(
    q_hbm, k_hbm, v_hbm, w_hbm, freq_hbm, len_hbm, out_ref,
    freq_ref, len_ref, q_in, k_in, v_in, in_sem, q_stage, kv_stage, qbuf, kv, start_ref, m_ref, l_ref, acc_ref, own_att, att, wbuf, pbuf, part,
    a_s, a_r, q_s, q_r, z_s, z_r, sh_s, sh_r, g_s, g_r, w_s, w_r, wsh_s, wsh_r, e_s, e_r,
):
    t = lax.axis_index("tok")
    y = lax.axis_index("feat")
    x = t // 16
    z = (t // 2) % NZ
    c = t % 2

    def device(dx, dz, dc):
        return (((x + dx) % NX) * 16 + ((z + dz) % NZ) * 2 + (c + dc) % 2, y)

    sibling = device(0, 0, 1)

    barrier = pltpu.get_barrier_semaphore()
    count = 0

    def greet(who):
        pl.semaphore_signal(barrier, inc=1, device_id=who, device_id_type=MESH)

    for dx in range(NX):
        for dy in range(NY):
            if dx or dy:
                greet((((x + dx) % NX) * 16 + z * 2 + c, (y + dy) % NY))
                count += 1
        greet(device(dx, 0, 1))
        count += 1
    for dz in (1, NZ - 1):
        greet(device(0, dz, 0))
        count += 1

    loads = [
        pltpu.make_async_copy(k_hbm, k_in, in_sem.at[0]),
        pltpu.make_async_copy(v_hbm, v_in, in_sem.at[1]),
        pltpu.make_async_copy(q_hbm, q_in, in_sem.at[2]),
        pltpu.make_async_copy(w_hbm, wbuf.at[z, c], in_sem.at[3]),
        pltpu.make_async_copy(freq_hbm, freq_ref, in_sem.at[4]),
        pltpu.make_async_copy(len_hbm, len_ref, in_sem.at[5]),
    ]
    for load in loads:
        load.start()

    def copy(src, dst, send, recv, who):
        return pltpu.make_async_remote_copy(
            src_ref=src, dst_ref=dst, send_sem=send, recv_sem=recv, device_id=who, device_id_type=MESH
        )

    loads[4].wait()
    loads[5].wait()
    ends = []
    end = len_ref[0]
    for number in range(5):
        ends.append(end)
        end = end + len_ref[number + 1]

    def first_token(token):
        start = jnp.zeros(token.shape, jnp.int32)
        for end in ends:
            start = jnp.where(token >= end, end, start)
        return start

    token = t * ROWS + lax.broadcasted_iota(jnp.int32, (ROWS, HD), 0)
    angles = (token - first_token(token)).astype(jnp.float32) * freq_ref[...]
    cosine = jnp.cos(angles)
    sine = jnp.sin(angles)
    sine = jnp.where(lax.broadcasted_iota(jnp.int32, (ROWS, HD), 1) < HD // 2, -sine, sine)

    def rotate(block):
        wide = block.astype(jnp.float32)
        return wide * cosine + pltpu.roll(wide, HD // 2, 1) * sine

    loads[0].wait()
    loads[1].wait()
    for head in range(2):
        columns = slice(head * HD, (head + 1) * HD)
        kv_stage[head, 0] = rotate(k_in[:, columns]).T.astype(jnp.bfloat16)
        kv_stage[head, 1] = v_in[:, columns]
    kv[x, z, c] = kv_stage[x // 2]

    pl.semaphore_wait(barrier, count)

    def x_copy(dx):
        to = (x + dx) % NX
        return copy(kv_stage.at[to // 2], kv.at[x, z, c], a_s.at[dx], a_r.at[dx], device(dx, 0, 0))

    def x_arrival(dx):
        slot = kv.at[(x + NX - dx) % NX, z, c]
        return copy(slot, slot, a_s.at[dx], a_r.at[dx], sibling)

    def order(j):
        return j + j // 2 - 2 * (j // 3)

    def block_of(j, r):
        return kv.at[(x + NX - order(j)) % NX, (z + r) % NZ, c]

    def ring_copy(j, r, to_r, dz):
        block = block_of(j, r)
        return copy(block, block, z_s.at[j, to_r], z_r.at[j, to_r], device(0, dz, 0))

    def share_copy(j, r):
        block = block_of(j, r)
        return copy(block, block, sh_s.at[j, r], sh_r.at[j, r], sibling)

    def share_arrival(j, r):
        block = kv.at[(x + NX - order(j)) % NX, (z + r) % NZ, 1 - c]
        return copy(block, block, sh_s.at[j, r], sh_r.at[j, r], sibling)

    def w_copy(r, to_r, dz):
        block = wbuf.at[(z + r) % NZ, c]
        return copy(block, block, w_s.at[to_r], w_r.at[to_r], device(0, dz, 0))

    def w_share(r):
        block = wbuf.at[(z + r) % NZ, c]
        return copy(block, block, wsh_s.at[r], wsh_r.at[r], sibling)

    def w_share_arrival(r):
        block = wbuf.at[(z + r) % NZ, 1 - c]
        return copy(block, block, wsh_s.at[r], wsh_r.at[r], sibling)

    for dx in (1, 3, 2):
        x_copy(dx).start()
    ring_copy(0, 0, 7, 1).start()
    ring_copy(0, 0, 1, NZ - 1).start()
    share_copy(0, 0).start()
    loads[3].wait()
    w_copy(0, 7, 1).start()
    w_copy(0, 1, NZ - 1).start()
    w_share(0).start()
    loads[2].wait()

    for head in range(8):
        q_stage[head] = rotate(q_in[:, head * HD : (head + 1) * HD]).astype(jnp.bfloat16)
    qbuf[x, c] = q_stage[2 * x + c]

    def q_copy(dx, dc):
        head = 2 * ((x + dx) % NX) + (c + dc) % 2
        return copy(q_stage.at[head], qbuf.at[x, c], q_s.at[dx, dc], q_r.at[dx, dc], device(dx, 0, dc))

    def q_arrival(dx, dc):
        slot = qbuf.at[(x + NX - dx) % NX, (c + dc) % 2]
        return copy(slot, slot, q_s.at[dx, dc], q_r.at[dx, dc], sibling)

    partners = [(0, 1), (1, 0), (1, 1), (3, 0), (3, 1), (2, 0), (2, 1)]
    for dx, dc in partners:
        q_copy(dx, dc).start()

    row_iota = lax.broadcasted_iota(jnp.int32, (2 * ROWS, HD), 0)

    def prepare(row, _):
        token = row * (16 * ROWS) + z * (2 * ROWS) + row_iota
        start_ref[row] = first_token(token)
        m_ref[row] = jnp.full((2 * ROWS, HD), LOW, jnp.float32)
        l_ref[row] = jnp.zeros((2 * ROWS, HD), jnp.float32)
        acc_ref[row] = jnp.zeros((2 * ROWS, HD), jnp.float32)
        return 0

    lax.fori_loop(0, NX, prepare, 0)

    for j, dx in ((1, 1), (2, 3), (3, 2)):
        x_arrival(dx).wait_recv()
        ring_copy(j, 0, 7, 1).start()
        ring_copy(j, 0, 1, NZ - 1).start()
        share_copy(j, 0).start()

    def attend_rows(rows, r):
        zk = (z + r) % NZ
        lane = lax.broadcasted_iota(jnp.int32, (2 * ROWS, HD), 1)
        keys = [
            jnp.concatenate([kv[xk, zk, 0, 0], kv[xk, zk, 1, 0]], axis=1)
            for xk in range(max(rows) + 1)
        ]
        scores = []
        for row in rows:
            q = qbuf[row].reshape(2 * ROWS, HD)
            scores.append(
                [jnp.dot(q, keys[xk], preferred_element_type=jnp.float32) for xk in range(row + 1)]
            )
        for row, raws in zip(rows, scores):
            start = start_ref[row]
            token = row * (16 * ROWS) + z * (2 * ROWS) + row_iota
            pieces = []
            for xk, raw in enumerate(raws):
                for side in range(2):
                    key = xk * (16 * ROWS) + zk * (2 * ROWS) + side * HD + lane
                    visible = key >= start
                    if xk == row:
                        visible = visible & (key <= token)
                    piece = raw[:, side * HD : (side + 1) * HD]
                    pieces.append(jnp.where(visible, piece, MASKED))
            old = m_ref[row]
            new = jnp.maximum(
                old, jnp.max(functools.reduce(jnp.maximum, pieces), axis=1, keepdims=True)
            )
            shrink = jnp.exp2((old - new) * FACTOR)
            weights = [jnp.exp2((piece - new) * FACTOR) for piece in pieces]
            m_ref[row] = new
            l_ref[row] = l_ref[row] * shrink + functools.reduce(jnp.add, weights)
            v = kv[0 : row + 1, zk, :, 1].reshape((row + 1) * 2 * ROWS, HD)
            acc_ref[row] = acc_ref[row] * shrink + jnp.dot(
                jnp.concatenate([weight.astype(jnp.bfloat16) for weight in weights], axis=1),
                v,
                preferred_element_type=jnp.float32,
            )

    def attend_unit(unit, _):
        group = unit // 2
        odd = group % 2
        d = (group + 1) // 2
        r = odd * (NZ - d) + (1 - odd) * d

        @pl.when(unit % 2 == 0)
        def _():
            for j in range(4):
                share_arrival(j, r).wait_recv()
            attend_rows((0, 3), r)

        @pl.when(unit % 2 == 1)
        def _():
            attend_rows((1, 2), r)

        return 0

    def item(m):
        d = 1 + m // 8
        j = (m // 2) % 4
        s = m % 2
        return d, j, s, (1 - s) * (NZ - d) + s * d

    def arrive(m):
        d, j, s, r = item(m)
        block = block_of(j, r)
        copy(block, block, z_s.at[j, r], z_r.at[j, r], sibling).wait_recv()

        @pl.when((d < 3) | (c == s))
        def _():
            ring_copy(j, r, r - 1 + 2 * s, (1 + 6 * s)).start()

        share_copy(j, r).start()

    def arrive_pair(p):
        arrive(2 * p)
        arrive(2 * p + 1)

    def hop(p, _):
        arrive_pair(p)
        return 0

    def w_step(n):
        d = 1 + n // 2
        s = n % 2
        r = (1 - s) * (NZ - d) + s * d
        block = wbuf.at[(z + r) % NZ, c]
        copy(block, block, w_s.at[r], w_r.at[r], sibling).wait_recv()

        @pl.when((d < 3) | (c == s))
        def _():
            w_copy(r, r - 1 + 2 * s, 1 + 6 * s).start()

        w_share(r).start()

    lax.fori_loop(0, 4, hop, 0)
    for dx, dc in partners:
        q_arrival(dx, dc).wait_recv()
    def first_unit(step):
        return step + (jnp.minimum(step, 3) + 1) // 2

    def ring_step(step, _):
        @pl.when(step < 8)
        def _():
            arrive_pair(step + 4)

        @pl.when(step == 8)
        def _():
            w_step(0)
            w_step(1)

        @pl.when((step >= 8) & (step < 12))
        def _():
            block = block_of(step - 8, 4)
            copy(block, block, z_s.at[step - 8, 4], z_r.at[step - 8, 4], sibling).wait_recv()
            share_copy(step - 8, 4).start()

        @pl.when(step == 12)
        def _():
            w_step(2)
            w_step(3)

        lax.fori_loop(first_unit(step), first_unit(step + 1), attend_unit, 0)
        return 0

    lax.fori_loop(0, 14, ring_step, 0)

    def finish(row, _):
        total = jnp.sum(l_ref[row], axis=1, keepdims=True)
        done = (acc_ref[row] / total).astype(jnp.bfloat16)
        own_att[0, row] = done[:ROWS]
        own_att[1, row] = done[ROWS:]
        return 0

    lax.fori_loop(0, NX, finish, 0)

    def g_slot(dx, dc, half):
        return att.at[2 * ((x + NX - dx) % NX) + (c + dc) % 2, 2 * half : 2 * half + 2]

    def g_copy(dx, dc, half):
        block = own_att.at[(c + dc) % 2, 2 * half : 2 * half + 2]
        return copy(
            block, g_slot(0, 0, half), g_s.at[dx, dc, half], g_r.at[dx, dc, half], device(dx, 0, dc)
        )

    def g_forward(dc, half):
        slot = g_slot(1 + 2 * half, dc, half)
        return copy(
            slot, slot, g_s.at[2, dc, half], g_r.at[2, dc, half], device(1 + 2 * half, 0, 0)
        )

    def g_arrival(dx, dc, half):
        slot = g_slot(dx, dc, half)
        return copy(slot, slot, g_s.at[dx, dc, half], g_r.at[dx, dc, half], sibling)

    onward = [(1, 0, 0), (3, 0, 1), (1, 1, 0), (3, 1, 1)]
    near = [(1, 0, 1), (3, 0, 0), (1, 1, 1), (3, 1, 0), (0, 1, 0), (0, 1, 1)]
    far = [(2, 0, 0), (2, 0, 1), (2, 1, 0), (2, 1, 1)]
    for place in onward + near:
        g_copy(*place).start()
    att[2 * x + c] = own_att[c]
    w_step(4)
    w_step(5)
    for dx, dc, half in onward:
        g_arrival(dx, dc, half).wait_recv()
        g_forward(dc, half).start()

    last_w = wbuf.at[(z + 4) % NZ, c]
    copy(last_w, last_w, w_s.at[4], w_r.at[4], sibling).wait_recv()
    w_share(4).start()

    for place in near + far:
        g_arrival(*place).wait_recv()

    def w_wait(r, _):
        w_share_arrival(r).wait_recv()
        return 0

    lax.fori_loop(0, NZ, w_wait, 0)

    def e_copy(row, nb):
        return copy(
            pbuf.at[row, nb], part.at[y, nb], e_s.at[row, nb], e_r.at[y, nb], (row * 16 + z * 2 + c, x)
        )

    def project(nb, _):
        left = jnp.concatenate([att[head].reshape(4 * ROWS, HD) for head in range(8)], axis=1)
        right = wbuf[pl.ds(2 * nb, 2)].reshape(2 * HD, 8 * HD)
        product = lax.dot_general(
            left, right, (((1,), (1,)), ((), ())), preferred_element_type=jnp.float32
        ).astype(jnp.bfloat16)
        for row in range(NX):
            pbuf[row, nb] = product[row * ROWS : (row + 1) * ROWS]
        for row in range(NX):
            mine = (x == row) & (y == x)

            @pl.when(mine)
            def _():
                part[y, nb] = pbuf[row, nb]

            @pl.when(jnp.logical_not(mine))
            def _():
                e_copy(row, nb).start()

        return 0

    lax.fori_loop(0, 4, project, 0)

    for nb in range(4):
        for source in range(NY):
            slot = part.at[source, nb]
            arrival = copy(slot, slot, e_s.at[source, nb], e_r.at[source, nb], sibling)

            @pl.when(jnp.logical_not((x == y) & (source == y)))
            def _():
                arrival.wait_recv()

        total = part[0, nb].astype(jnp.float32)
        for source in range(1, NY):
            total = total + part[source, nb].astype(jnp.float32)
        out_ref[:, nb * 256 : (nb + 1) * 256] = total.astype(jnp.bfloat16)

    for dx in (1, 3, 2):
        x_copy(dx).wait_send()
    for dx, dc in partners:
        q_copy(dx, dc).wait_send()
    for place in onward + near:
        g_copy(*place).wait_send()
    for _, dc, half in far:
        g_forward(dc, half).wait_send()

    def sent(n, _):
        j = n % 4
        r = n // 4
        share_copy(j, r).wait_send()
        return 0

    lax.fori_loop(0, 32, sent, 0)

    def ring_sent(n, _):
        j = n % 4
        r = 1 + n // 4
        block = block_of(j, r)
        copy(block, block, z_s.at[j, r], z_r.at[j, r], sibling).wait_send()
        return 0

    lax.fori_loop(0, 28, ring_sent, 0)

    def w_sent(r, _):
        w_share(r).wait_send()
        return 0

    lax.fori_loop(0, NZ, w_sent, 0)

    def w_ring_sent(r, _):
        block = wbuf.at[(z + r) % NZ, c]
        copy(block, block, w_s.at[r], w_r.at[r], sibling).wait_send()
        return 0

    lax.fori_loop(1, NZ, w_ring_sent, 0)
    for row in range(NX):
        mine = (x == row) & (y == x)

        @pl.when(jnp.logical_not(mine))
        def _():
            for nb in range(4):
                e_copy(row, nb).wait_send()


def shards(queries, keys, values, out_weight, doc_lengths):
    vmem = pl.BlockSpec(memory_space=pltpu.VMEM)
    hbm = pl.BlockSpec(memory_space=pltpu.HBM)
    bf16, f32 = jnp.bfloat16, jnp.float32
    dma = pltpu.SemaphoreType.DMA
    operands = (queries, keys, values, out_weight.T, jnp.asarray(frequencies()), doc_lengths)
    return pl.pallas_call(
        kernel,
        out_shape=jax.ShapeDtypeStruct((ROWS, 1024), bf16),
        in_specs=[hbm] * 6,
        out_specs=vmem,
        scratch_shapes=[
            pltpu.VMEM((1, HD), f32),
            pltpu.SMEM((6,), jnp.int32),
            pltpu.VMEM((ROWS, 1024), bf16),
            pltpu.VMEM((ROWS, 256), bf16),
            pltpu.VMEM((ROWS, 256), bf16),
            dma((6,)),
            pltpu.VMEM((8, ROWS, HD), bf16),
            pltpu.VMEM((2, 2, ROWS, HD), bf16),
            pltpu.VMEM((NX, 2, ROWS, HD), bf16),
            pltpu.VMEM((NX, NZ, 2, 2, ROWS, HD), bf16),
            pltpu.VMEM((NX, 2 * ROWS, HD), jnp.int32),
            pltpu.VMEM((NX, 2 * ROWS, HD), f32),
            pltpu.VMEM((NX, 2 * ROWS, HD), f32),
            pltpu.VMEM((NX, 2 * ROWS, HD), f32),
            pltpu.VMEM((2, NX, ROWS, HD), bf16),
            pltpu.VMEM((8, NX, ROWS, HD), bf16),
            pltpu.VMEM((NZ, 2, 64, 1024), bf16),
            pltpu.VMEM((NX, 4, ROWS, 256), bf16),
            pltpu.VMEM((NY, 4, ROWS, 256), bf16),
            dma((4,)), dma((4,)),
            dma((4, 2)), dma((4, 2)),
            dma((4, 8)), dma((4, 8)),
            dma((4, 8)), dma((4, 8)),
            dma((4, 2, 2)), dma((4, 2, 2)),
            dma((8,)), dma((8,)),
            dma((8,)), dma((8,)),
            dma((4, 4)), dma((4, 4)),
        ],
        compiler_params=pltpu.CompilerParams(
            collective_id=0, has_side_effects=True, vmem_limit_bytes=48 << 20
        ),
    )(*(pltpu.with_memory_space_constraint(array, pltpu.HBM) for array in operands))


def solution(mesh):
    in_specs = (P("tok", "feat"), P("tok", "feat"), P("tok", "feat"), P("feat", "tok"), P())
    return jax.shard_map(
        shards, mesh=mesh, in_specs=in_specs, out_specs=P("tok", "feat"), check_vma=False
    )
```

```python
import functools

import jax
import jax.numpy as jnp
import numpy as np
from jax import lax
from jax.experimental import pallas as pl
from jax.experimental.pallas import tpu as pltpu
from jax.sharding import PartitionSpec as P

HD = 128
ROPE_BASE = 500000.0
LOW = -1e30
MASKED = -2e30
ROWS = 128
NX, NZ, NY = 4, 8, 4
FACTOR = float(HD**-0.5 * np.log2(np.e))
MESH = pl.DeviceIdType.MESH


def frequencies():
    half = HD // 2
    frequency = ROPE_BASE ** (-(np.arange(half, dtype=np.float64) * 2.0 / HD))
    return np.concatenate([frequency, frequency]).astype(np.float32).reshape(1, HD)


def kernel(
    q_hbm, k_hbm, v_hbm, w_hbm, freq_hbm, len_hbm, out_ref,
    freq_ref, len_ref, q_in, k_in, v_in, in_sem, q_stage, kv_stage, qbuf, kv, start_ref, m_ref, l_ref, acc_ref, own_att, att, wbuf, pbuf, part,
    a_s, a_r, q_s, q_r, z_s, z_r, sh_s, sh_r, g_s, g_r, w_s, w_r, wsh_s, wsh_r, e_s, e_r,
):
    t = lax.axis_index("tok")
    y = lax.axis_index("feat")
    x = t // 16
    z = (t // 2) % NZ
    c = t % 2

    def device(dx, dz, dc):
        return (((x + dx) % NX) * 16 + ((z + dz) % NZ) * 2 + (c + dc) % 2, y)

    sibling = device(0, 0, 1)

    barrier = pltpu.get_barrier_semaphore()
    count = 0

    def greet(who):
        pl.semaphore_signal(barrier, inc=1, device_id=who, device_id_type=MESH)

    for dx in range(NX):
        for dy in range(NY):
            if dx or dy:
                greet((((x + dx) % NX) * 16 + z * 2 + c, (y + dy) % NY))
                count += 1
        greet(device(dx, 0, 1))
        count += 1
    for dz in (1, NZ - 1):
        greet(device(0, dz, 0))
        count += 1

    loads = [
        pltpu.make_async_copy(k_hbm, k_in, in_sem.at[0]),
        pltpu.make_async_copy(v_hbm, v_in, in_sem.at[1]),
        pltpu.make_async_copy(q_hbm, q_in, in_sem.at[2]),
        pltpu.make_async_copy(w_hbm, wbuf.at[z, c], in_sem.at[3]),
        pltpu.make_async_copy(freq_hbm, freq_ref, in_sem.at[4]),
        pltpu.make_async_copy(len_hbm, len_ref, in_sem.at[5]),
    ]
    for load in loads:
        load.start()

    def copy(src, dst, send, recv, who):
        return pltpu.make_async_remote_copy(
            src_ref=src, dst_ref=dst, send_sem=send, recv_sem=recv, device_id=who, device_id_type=MESH
        )

    loads[4].wait()
    loads[5].wait()
    ends = []
    end = len_ref[0]
    for number in range(5):
        ends.append(end)
        end = end + len_ref[number + 1]

    def first_token(token):
        start = jnp.zeros(token.shape, jnp.int32)
        for end in ends:
            start = jnp.where(token >= end, end, start)
        return start

    token = t * ROWS + lax.broadcasted_iota(jnp.int32, (ROWS, HD), 0)
    angles = (token - first_token(token)).astype(jnp.float32) * freq_ref[...]
    cosine = jnp.cos(angles)
    sine = jnp.sin(angles)
    sine = jnp.where(lax.broadcasted_iota(jnp.int32, (ROWS, HD), 1) < HD // 2, -sine, sine)

    def rotate(block):
        wide = block.astype(jnp.float32)
        return wide * cosine + pltpu.roll(wide, HD // 2, 1) * sine

    loads[0].wait()
    loads[1].wait()
    for head in range(2):
        columns = slice(head * HD, (head + 1) * HD)
        kv_stage[head, 0] = rotate(k_in[:, columns]).T.astype(jnp.bfloat16)
        kv_stage[head, 1] = v_in[:, columns]
    kv[x, z, c] = kv_stage[x // 2]

    pl.semaphore_wait(barrier, count)

    def x_copy(dx):
        to = (x + dx) % NX
        return copy(kv_stage.at[to // 2], kv.at[x, z, c], a_s.at[dx], a_r.at[dx], device(dx, 0, 0))

    def x_arrival(dx):
        slot = kv.at[(x + NX - dx) % NX, z, c]
        return copy(slot, slot, a_s.at[dx], a_r.at[dx], sibling)

    def order(j):
        return j + j // 2 - 2 * (j // 3)

    def block_of(j, r):
        return kv.at[(x + NX - order(j)) % NX, (z + r) % NZ, c]

    def ring_copy(j, r, to_r, dz):
        block = block_of(j, r)
        return copy(block, block, z_s.at[j, to_r], z_r.at[j, to_r], device(0, dz, 0))

    def share_copy(j, r):
        block = block_of(j, r)
        return copy(block, block, sh_s.at[j, r], sh_r.at[j, r], sibling)

    def share_arrival(j, r):
        block = kv.at[(x + NX - order(j)) % NX, (z + r) % NZ, 1 - c]
        return copy(block, block, sh_s.at[j, r], sh_r.at[j, r], sibling)

    def w_copy(r, to_r, dz):
        block = wbuf.at[(z + r) % NZ, c]
        return copy(block, block, w_s.at[to_r], w_r.at[to_r], device(0, dz, 0))

    def w_share(r):
        block = wbuf.at[(z + r) % NZ, c]
        return copy(block, block, wsh_s.at[r], wsh_r.at[r], sibling)

    def w_share_arrival(r):
        block = wbuf.at[(z + r) % NZ, 1 - c]
        return copy(block, block, wsh_s.at[r], wsh_r.at[r], sibling)

    for dx in (1, 3, 2):
        x_copy(dx).start()
    ring_copy(0, 0, 7, 1).start()
    ring_copy(0, 0, 1, NZ - 1).start()
    share_copy(0, 0).start()
    loads[3].wait()
    w_copy(0, 7, 1).start()
    w_copy(0, 1, NZ - 1).start()
    w_share(0).start()
    loads[2].wait()

    for head in range(8):
        q_stage[head] = rotate(q_in[:, head * HD : (head + 1) * HD]).astype(jnp.bfloat16)
    qbuf[x, c] = q_stage[2 * x + c]

    def q_copy(dx, dc):
        head = 2 * ((x + dx) % NX) + (c + dc) % 2
        return copy(q_stage.at[head], qbuf.at[x, c], q_s.at[dx, dc], q_r.at[dx, dc], device(dx, 0, dc))

    def q_arrival(dx, dc):
        slot = qbuf.at[(x + NX - dx) % NX, (c + dc) % 2]
        return copy(slot, slot, q_s.at[dx, dc], q_r.at[dx, dc], sibling)

    partners = [(0, 1), (1, 0), (1, 1), (3, 0), (3, 1), (2, 0), (2, 1)]
    for dx, dc in partners:
        q_copy(dx, dc).start()

    row_iota = lax.broadcasted_iota(jnp.int32, (2 * ROWS, HD), 0)

    def prepare(row, _):
        token = row * (16 * ROWS) + z * (2 * ROWS) + row_iota
        start_ref[row] = first_token(token)
        m_ref[row] = jnp.full((2 * ROWS, HD), LOW, jnp.float32)
        l_ref[row] = jnp.zeros((2 * ROWS, HD), jnp.float32)
        acc_ref[row] = jnp.zeros((2 * ROWS, HD), jnp.float32)
        return 0

    lax.fori_loop(0, NX, prepare, 0)

    for j, dx in ((1, 1), (2, 3), (3, 2)):
        x_arrival(dx).wait_recv()
        ring_copy(j, 0, 7, 1).start()
        ring_copy(j, 0, 1, NZ - 1).start()
        share_copy(j, 0).start()

    def attend_rows(rows, r):
        zk = (z + r) % NZ
        lane = lax.broadcasted_iota(jnp.int32, (2 * ROWS, HD), 1)
        keys = [
            jnp.concatenate([kv[xk, zk, 0, 0], kv[xk, zk, 1, 0]], axis=1)
            for xk in range(max(rows) + 1)
        ]
        scores = []
        for row in rows:
            q = qbuf[row].reshape(2 * ROWS, HD)
            scores.append(
                [jnp.dot(q, keys[xk], preferred_element_type=jnp.float32) for xk in range(row + 1)]
            )
        for row, raws in zip(rows, scores):
            start = start_ref[row]
            token = row * (16 * ROWS) + z * (2 * ROWS) + row_iota
            pieces = []
            for xk, raw in enumerate(raws):
                for side in range(2):
                    key = xk * (16 * ROWS) + zk * (2 * ROWS) + side * HD + lane
                    visible = key >= start
                    if xk == row:
                        visible = visible & (key <= token)
                    piece = raw[:, side * HD : (side + 1) * HD]
                    pieces.append(jnp.where(visible, piece, MASKED))
            old = m_ref[row]
            new = jnp.maximum(
                old, jnp.max(functools.reduce(jnp.maximum, pieces), axis=1, keepdims=True)
            )
            shrink = jnp.exp2((old - new) * FACTOR)
            weights = [jnp.exp2((piece - new) * FACTOR) for piece in pieces]
            m_ref[row] = new
            l_ref[row] = l_ref[row] * shrink + functools.reduce(jnp.add, weights)
            v = kv[0 : row + 1, zk, :, 1].reshape((row + 1) * 2 * ROWS, HD)
            acc_ref[row] = acc_ref[row] * shrink + jnp.dot(
                jnp.concatenate([weight.astype(jnp.bfloat16) for weight in weights], axis=1),
                v,
                preferred_element_type=jnp.float32,
            )

    def attend_unit(unit, _):
        group = unit // 2
        odd = group % 2
        d = (group + 1) // 2
        r = odd * (NZ - d) + (1 - odd) * d

        @pl.when(unit % 2 == 0)
        def _():
            for j in range(4):
                share_arrival(j, r).wait_recv()
            attend_rows((0, 3), r)

        @pl.when(unit % 2 == 1)
        def _():
            attend_rows((1, 2), r)

        return 0

    def item(m):
        d = 1 + m // 8
        j = (m // 2) % 4
        s = m % 2
        return d, j, s, (1 - s) * (NZ - d) + s * d

    def arrive(m):
        d, j, s, r = item(m)
        block = block_of(j, r)
        copy(block, block, z_s.at[j, r], z_r.at[j, r], sibling).wait_recv()

        @pl.when((d < 3) | (c == s))
        def _():
            ring_copy(j, r, r - 1 + 2 * s, (1 + 6 * s)).start()

        share_copy(j, r).start()

    def arrive_pair(p):
        arrive(2 * p)
        arrive(2 * p + 1)

    def hop(p, _):
        arrive_pair(p)
        return 0

    def w_step(n):
        d = 1 + n // 2
        s = n % 2
        r = (1 - s) * (NZ - d) + s * d
        block = wbuf.at[(z + r) % NZ, c]
        copy(block, block, w_s.at[r], w_r.at[r], sibling).wait_recv()

        @pl.when((d < 3) | (c == s))
        def _():
            w_copy(r, r - 1 + 2 * s, 1 + 6 * s).start()

        w_share(r).start()

    lax.fori_loop(0, 4, hop, 0)
    for dx, dc in partners:
        q_arrival(dx, dc).wait_recv()
    def first_unit(step):
        return step + (jnp.minimum(step, 3) + 1) // 2

    def ring_step(step, _):
        @pl.when(step < 8)
        def _():
            arrive_pair(step + 4)

        @pl.when(step == 8)
        def _():
            w_step(0)
            w_step(1)

        @pl.when((step >= 8) & (step < 12))
        def _():
            block = block_of(step - 8, 4)
            copy(block, block, z_s.at[step - 8, 4], z_r.at[step - 8, 4], sibling).wait_recv()
            share_copy(step - 8, 4).start()

        @pl.when(step == 12)
        def _():
            w_step(2)
            w_step(3)

        lax.fori_loop(first_unit(step), first_unit(step + 1), attend_unit, 0)
        return 0

    lax.fori_loop(0, 14, ring_step, 0)

    def finish(row, _):
        total = jnp.sum(l_ref[row], axis=1, keepdims=True)
        done = (acc_ref[row] / total).astype(jnp.bfloat16)
        own_att[0, row] = done[:ROWS]
        own_att[1, row] = done[ROWS:]
        return 0

    lax.fori_loop(0, NX, finish, 0)

    def g_slot(dx, dc, half):
        return att.at[2 * ((x + NX - dx) % NX) + (c + dc) % 2, 2 * half : 2 * half + 2]

    def g_copy(dx, dc, half):
        block = own_att.at[(c + dc) % 2, 2 * half : 2 * half + 2]
        return copy(
            block, g_slot(0, 0, half), g_s.at[dx, dc, half], g_r.at[dx, dc, half], device(dx, 0, dc)
        )

    def g_forward(dc, half):
        slot = g_slot(1 + 2 * half, dc, half)
        return copy(
            slot, slot, g_s.at[2, dc, half], g_r.at[2, dc, half], device(1 + 2 * half, 0, 0)
        )

    def g_arrival(dx, dc, half):
        slot = g_slot(dx, dc, half)
        return copy(slot, slot, g_s.at[dx, dc, half], g_r.at[dx, dc, half], sibling)

    onward = [(1, 0, 0), (3, 0, 1), (1, 1, 0), (3, 1, 1)]
    near = [(1, 0, 1), (3, 0, 0), (1, 1, 1), (3, 1, 0), (0, 1, 0), (0, 1, 1)]
    far = [(2, 0, 0), (2, 0, 1), (2, 1, 0), (2, 1, 1)]
    for place in onward + near:
        g_copy(*place).start()
    att[2 * x + c] = own_att[c]
    w_step(4)
    w_step(5)
    for dx, dc, half in onward:
        g_arrival(dx, dc, half).wait_recv()
        g_forward(dc, half).start()

    last_w = wbuf.at[(z + 4) % NZ, c]
    copy(last_w, last_w, w_s.at[4], w_r.at[4], sibling).wait_recv()
    w_share(4).start()

    for place in near + far:
        g_arrival(*place).wait_recv()

    def w_wait(r, _):
        w_share_arrival(r).wait_recv()
        return 0

    lax.fori_loop(0, NZ, w_wait, 0)

    def e_copy(row, nb):
        return copy(
            pbuf.at[row, nb], part.at[y, nb], e_s.at[row, nb], e_r.at[y, nb], (row * 16 + z * 2 + c, x)
        )

    def project(nb, _):
        left = jnp.concatenate([att[head].reshape(4 * ROWS, HD) for head in range(8)], axis=1)
        right = wbuf[pl.ds(2 * nb, 2)].reshape(2 * HD, 8 * HD)
        product = lax.dot_general(
            left, right, (((1,), (1,)), ((), ())), preferred_element_type=jnp.float32
        ).astype(jnp.bfloat16)
        for row in range(NX):
            pbuf[row, nb] = product[row * ROWS : (row + 1) * ROWS]
        for row in range(NX):
            mine = (x == row) & (y == x)

            @pl.when(mine)
            def _():
                part[y, nb] = pbuf[row, nb]

            @pl.when(jnp.logical_not(mine))
            def _():
                e_copy(row, nb).start()

        return 0

    lax.fori_loop(0, 4, project, 0)

    for dx in (1, 3, 2):
        x_copy(dx).wait_send()
    for dx, dc in partners:
        q_copy(dx, dc).wait_send()
    for place in onward + near:
        g_copy(*place).wait_send()
    for _, dc, half in far:
        g_forward(dc, half).wait_send()

    def sent(n, _):
        j = n % 4
        r = n // 4
        share_copy(j, r).wait_send()
        return 0

    lax.fori_loop(0, 32, sent, 0)

    def ring_sent(n, _):
        j = n % 4
        r = 1 + n // 4
        block = block_of(j, r)
        copy(block, block, z_s.at[j, r], z_r.at[j, r], sibling).wait_send()
        return 0

    lax.fori_loop(0, 28, ring_sent, 0)

    def w_sent(r, _):
        w_share(r).wait_send()
        return 0

    lax.fori_loop(0, NZ, w_sent, 0)

    def w_ring_sent(r, _):
        block = wbuf.at[(z + r) % NZ, c]
        copy(block, block, w_s.at[r], w_r.at[r], sibling).wait_send()
        return 0

    lax.fori_loop(1, NZ, w_ring_sent, 0)
    for nb in range(4):
        for source in range(NY):
            slot = part.at[source, nb]
            arrival = copy(slot, slot, e_s.at[source, nb], e_r.at[source, nb], sibling)

            @pl.when(jnp.logical_not((x == y) & (source == y)))
            def _():
                arrival.wait_recv()

        total = part[0, nb].astype(jnp.float32)
        for source in range(1, NY):
            total = total + part[source, nb].astype(jnp.float32)
        out_ref[:, nb * 256 : (nb + 1) * 256] = total.astype(jnp.bfloat16)

    for row in range(NX):
        mine = (x == row) & (y == x)

        @pl.when(jnp.logical_not(mine))
        def _():
            for nb in range(4):
                e_copy(row, nb).wait_send()


def shards(queries, keys, values, out_weight, doc_lengths):
    vmem = pl.BlockSpec(memory_space=pltpu.VMEM)
    hbm = pl.BlockSpec(memory_space=pltpu.HBM)
    bf16, f32 = jnp.bfloat16, jnp.float32
    dma = pltpu.SemaphoreType.DMA
    operands = (queries, keys, values, out_weight.T, jnp.asarray(frequencies()), doc_lengths)
    return pl.pallas_call(
        kernel,
        out_shape=jax.ShapeDtypeStruct((ROWS, 1024), bf16),
        in_specs=[hbm] * 6,
        out_specs=vmem,
        scratch_shapes=[
            pltpu.VMEM((1, HD), f32),
            pltpu.SMEM((6,), jnp.int32),
            pltpu.VMEM((ROWS, 1024), bf16),
            pltpu.VMEM((ROWS, 256), bf16),
            pltpu.VMEM((ROWS, 256), bf16),
            dma((6,)),
            pltpu.VMEM((8, ROWS, HD), bf16),
            pltpu.VMEM((2, 2, ROWS, HD), bf16),
            pltpu.VMEM((NX, 2, ROWS, HD), bf16),
            pltpu.VMEM((NX, NZ, 2, 2, ROWS, HD), bf16),
            pltpu.VMEM((NX, 2 * ROWS, HD), jnp.int32),
            pltpu.VMEM((NX, 2 * ROWS, HD), f32),
            pltpu.VMEM((NX, 2 * ROWS, HD), f32),
            pltpu.VMEM((NX, 2 * ROWS, HD), f32),
            pltpu.VMEM((2, NX, ROWS, HD), bf16),
            pltpu.VMEM((8, NX, ROWS, HD), bf16),
            pltpu.VMEM((NZ, 2, 64, 1024), bf16),
            pltpu.VMEM((NX, 4, ROWS, 256), bf16),
            pltpu.VMEM((NY, 4, ROWS, 256), bf16),
            dma((4,)), dma((4,)),
            dma((4, 2)), dma((4, 2)),
            dma((4, 8)), dma((4, 8)),
            dma((4, 8)), dma((4, 8)),
            dma((4, 2, 2)), dma((4, 2, 2)),
            dma((8,)), dma((8,)),
            dma((8,)), dma((8,)),
            dma((4, 4)), dma((4, 4)),
        ],
        compiler_params=pltpu.CompilerParams(
            collective_id=0, has_side_effects=True, vmem_limit_bytes=48 << 20
        ),
    )(*(pltpu.with_memory_space_constraint(array, pltpu.HBM) for array in operands))


def solution(mesh):
    in_specs = (P("tok", "feat"), P("tok", "feat"), P("tok", "feat"), P("feat", "tok"), P())
    return jax.shard_map(
        shards, mesh=mesh, in_specs=in_specs, out_specs=P("tok", "feat"), check_vma=False
    )
```

```python
import functools

import jax
import jax.numpy as jnp
import numpy as np
from jax import lax
from jax.experimental import pallas as pl
from jax.experimental.pallas import tpu as pltpu
from jax.sharding import PartitionSpec as P

HD = 128
ROPE_BASE = 500000.0
LOW = -1e30
MASKED = -2e30
ROWS = 128
NX, NZ, NY = 4, 8, 4
FACTOR = float(HD**-0.5 * np.log2(np.e))
MESH = pl.DeviceIdType.MESH


def frequencies():
    half = HD // 2
    frequency = ROPE_BASE ** (-(np.arange(half, dtype=np.float64) * 2.0 / HD))
    return np.concatenate([frequency, frequency]).astype(np.float32).reshape(1, HD)


def kernel(
    q_hbm, k_hbm, v_hbm, w_hbm, freq_hbm, len_hbm, out_ref,
    freq_ref, len_ref, q_in, k_in, v_in, in_sem, q_stage, kv_stage, qbuf, kv, start_ref, m_ref, l_ref, acc_ref, own_att, att, wbuf, pbuf, part,
    a_s, a_r, q_s, q_r, z_s, z_r, sh_s, sh_r, g_s, g_r, w_s, w_r, wsh_s, wsh_r, e_s, e_r,
):
    t = lax.axis_index("tok")
    y = lax.axis_index("feat")
    x = t // 16
    z = (t // 2) % NZ
    c = t % 2

    def device(dx, dz, dc):
        return (((x + dx) % NX) * 16 + ((z + dz) % NZ) * 2 + (c + dc) % 2, y)

    sibling = device(0, 0, 1)

    barrier = pltpu.get_barrier_semaphore()
    count = 0

    def greet(who):
        pl.semaphore_signal(barrier, inc=1, device_id=who, device_id_type=MESH)

    for dx in range(NX):
        for dy in range(NY):
            if dx or dy:
                greet((((x + dx) % NX) * 16 + z * 2 + c, (y + dy) % NY))
                count += 1
        greet(device(dx, 0, 1))
        count += 1
    for dz in (1, NZ - 1):
        greet(device(0, dz, 0))
        count += 1

    loads = [
        pltpu.make_async_copy(k_hbm, k_in, in_sem.at[0]),
        pltpu.make_async_copy(v_hbm, v_in, in_sem.at[1]),
        pltpu.make_async_copy(q_hbm, q_in, in_sem.at[2]),
        pltpu.make_async_copy(w_hbm, wbuf.at[z, c], in_sem.at[3]),
        pltpu.make_async_copy(freq_hbm, freq_ref, in_sem.at[4]),
        pltpu.make_async_copy(len_hbm, len_ref, in_sem.at[5]),
    ]
    for load in loads:
        load.start()

    def copy(src, dst, send, recv, who):
        return pltpu.make_async_remote_copy(
            src_ref=src, dst_ref=dst, send_sem=send, recv_sem=recv, device_id=who, device_id_type=MESH
        )

    loads[4].wait()
    loads[5].wait()
    ends = []
    end = len_ref[0]
    for number in range(5):
        ends.append(end)
        end = end + len_ref[number + 1]

    def first_token(token):
        start = jnp.zeros(token.shape, jnp.int32)
        for end in ends:
            start = jnp.where(token >= end, end, start)
        return start

    token = t * ROWS + lax.broadcasted_iota(jnp.int32, (ROWS, HD), 0)
    angles = (token - first_token(token)).astype(jnp.float32) * freq_ref[...]
    cosine = jnp.cos(angles)
    sine = jnp.sin(angles)
    sine = jnp.where(lax.broadcasted_iota(jnp.int32, (ROWS, HD), 1) < HD // 2, -sine, sine)

    def rotate(block):
        wide = block.astype(jnp.float32)
        return wide * cosine + pltpu.roll(wide, HD // 2, 1) * sine

    loads[0].wait()
    loads[1].wait()
    for head in range(2):
        columns = slice(head * HD, (head + 1) * HD)
        kv_stage[head, 0] = rotate(k_in[:, columns]).T.astype(jnp.bfloat16)
        kv_stage[head, 1] = v_in[:, columns]
    kv[x, z, c] = kv_stage[x // 2]

    pl.semaphore_wait(barrier, count)

    def x_copy(dx):
        to = (x + dx) % NX
        return copy(kv_stage.at[to // 2], kv.at[x, z, c], a_s.at[dx], a_r.at[dx], device(dx, 0, 0))

    def x_arrival(dx):
        slot = kv.at[(x + NX - dx) % NX, z, c]
        return copy(slot, slot, a_s.at[dx], a_r.at[dx], sibling)

    def order(j):
        return j + j // 2 - 2 * (j // 3)

    def block_of(j, r):
        return kv.at[(x + NX - order(j)) % NX, (z + r) % NZ, c]

    def ring_copy(j, r, to_r, dz):
        block = block_of(j, r)
        return copy(block, block, z_s.at[j, to_r], z_r.at[j, to_r], device(0, dz, 0))

    def share_copy(j, r):
        block = block_of(j, r)
        return copy(block, block, sh_s.at[j, r], sh_r.at[j, r], sibling)

    def share_arrival(j, r):
        block = kv.at[(x + NX - order(j)) % NX, (z + r) % NZ, 1 - c]
        return copy(block, block, sh_s.at[j, r], sh_r.at[j, r], sibling)

    def w_copy(r, to_r, dz):
        block = wbuf.at[(z + r) % NZ, c]
        return copy(block, block, w_s.at[to_r], w_r.at[to_r], device(0, dz, 0))

    def w_share(r):
        block = wbuf.at[(z + r) % NZ, c]
        return copy(block, block, wsh_s.at[r], wsh_r.at[r], sibling)

    def w_share_arrival(r):
        block = wbuf.at[(z + r) % NZ, 1 - c]
        return copy(block, block, wsh_s.at[r], wsh_r.at[r], sibling)

    for dx in (1, 3, 2):
        x_copy(dx).start()
    ring_copy(0, 0, 7, 1).start()
    ring_copy(0, 0, 1, NZ - 1).start()
    share_copy(0, 0).start()
    loads[3].wait()
    w_copy(0, 7, 1).start()
    w_copy(0, 1, NZ - 1).start()
    w_share(0).start()
    loads[2].wait()

    for head in range(8):
        q_stage[head] = rotate(q_in[:, head * HD : (head + 1) * HD]).astype(jnp.bfloat16)
    qbuf[x, c] = q_stage[2 * x + c]

    def q_copy(dx, dc):
        head = 2 * ((x + dx) % NX) + (c + dc) % 2
        return copy(q_stage.at[head], qbuf.at[x, c], q_s.at[dx, dc], q_r.at[dx, dc], device(dx, 0, dc))

    def q_arrival(dx, dc):
        slot = qbuf.at[(x + NX - dx) % NX, (c + dc) % 2]
        return copy(slot, slot, q_s.at[dx, dc], q_r.at[dx, dc], sibling)

    partners = [(0, 1), (1, 0), (1, 1), (3, 0), (3, 1), (2, 0), (2, 1)]
    for dx, dc in partners:
        q_copy(dx, dc).start()

    row_iota = lax.broadcasted_iota(jnp.int32, (2 * ROWS, HD), 0)

    def prepare(row, _):
        token = row * (16 * ROWS) + z * (2 * ROWS) + row_iota
        start_ref[row] = first_token(token)
        m_ref[row] = jnp.full((2 * ROWS, HD), LOW, jnp.float32)
        l_ref[row] = jnp.zeros((2 * ROWS, HD), jnp.float32)
        acc_ref[row] = jnp.zeros((2 * ROWS, HD), jnp.float32)
        return 0

    lax.fori_loop(0, NX, prepare, 0)

    for j, dx in ((1, 1), (2, 3), (3, 2)):
        x_arrival(dx).wait_recv()
        ring_copy(j, 0, 7, 1).start()
        ring_copy(j, 0, 1, NZ - 1).start()
        share_copy(j, 0).start()

    def attend_rows(rows, r):
        zk = (z + r) % NZ
        lane = lax.broadcasted_iota(jnp.int32, (2 * ROWS, HD), 1)
        keys = [
            jnp.concatenate([kv[xk, zk, 0, 0], kv[xk, zk, 1, 0]], axis=1)
            for xk in range(max(rows) + 1)
        ]
        scores = []
        for row in rows:
            q = qbuf[row].reshape(2 * ROWS, HD)
            scores.append(
                [jnp.dot(q, keys[xk], preferred_element_type=jnp.float32) for xk in range(row + 1)]
            )
        for row, raws in zip(rows, scores):
            start = start_ref[row]
            token = row * (16 * ROWS) + z * (2 * ROWS) + row_iota
            pieces = []
            for xk, raw in enumerate(raws):
                for side in range(2):
                    key = xk * (16 * ROWS) + zk * (2 * ROWS) + side * HD + lane
                    visible = key >= start
                    if xk == row:
                        visible = visible & (key <= token)
                    piece = raw[:, side * HD : (side + 1) * HD]
                    pieces.append(jnp.where(visible, piece, MASKED))
            old = m_ref[row]
            new = jnp.maximum(
                old, jnp.max(functools.reduce(jnp.maximum, pieces), axis=1, keepdims=True)
            )
            shrink = jnp.exp2((old - new) * FACTOR)
            weights = [jnp.exp2((piece - new) * FACTOR) for piece in pieces]
            m_ref[row] = new
            l_ref[row] = l_ref[row] * shrink + functools.reduce(jnp.add, weights)
            v = kv[0 : row + 1, zk, :, 1].reshape((row + 1) * 2 * ROWS, HD)
            acc_ref[row] = acc_ref[row] * shrink + jnp.dot(
                jnp.concatenate([weight.astype(jnp.bfloat16) for weight in weights], axis=1),
                v,
                preferred_element_type=jnp.float32,
            )

    def attend_unit(unit, _):
        group = unit // 2
        odd = group % 2
        d = (group + 1) // 2
        r = odd * (NZ - d) + (1 - odd) * d

        @pl.when(unit % 2 == 0)
        def _():
            for j in range(4):
                share_arrival(j, r).wait_recv()
            attend_rows((0, 3), r)

        @pl.when(unit % 2 == 1)
        def _():
            attend_rows((1, 2), r)

        return 0

    def item(m):
        d = 1 + m // 8
        j = (m // 2) % 4
        s = m % 2
        return d, j, s, (1 - s) * (NZ - d) + s * d

    def arrive(m):
        d, j, s, r = item(m)
        block = block_of(j, r)
        copy(block, block, z_s.at[j, r], z_r.at[j, r], sibling).wait_recv()

        @pl.when((d < 3) | (c == s))
        def _():
            ring_copy(j, r, r - 1 + 2 * s, (1 + 6 * s)).start()

        share_copy(j, r).start()

    def arrive_pair(p):
        arrive(2 * p)
        arrive(2 * p + 1)

    def hop(p, _):
        arrive_pair(p)
        return 0

    def w_step(n):
        d = 1 + n // 2
        s = n % 2
        r = (1 - s) * (NZ - d) + s * d
        block = wbuf.at[(z + r) % NZ, c]
        copy(block, block, w_s.at[r], w_r.at[r], sibling).wait_recv()

        @pl.when((d < 3) | (c == s))
        def _():
            w_copy(r, r - 1 + 2 * s, 1 + 6 * s).start()

        w_share(r).start()

    lax.fori_loop(0, 4, hop, 0)
    for dx, dc in partners:
        q_arrival(dx, dc).wait_recv()
    def first_unit(step):
        return step + (jnp.minimum(step, 3) + 1) // 2

    def ring_step(step, _):
        @pl.when(step < 8)
        def _():
            arrive_pair(step + 4)

        @pl.when(step == 8)
        def _():
            w_step(0)
            w_step(1)

        @pl.when((step >= 8) & (step < 12))
        def _():
            block = block_of(step - 8, 4)
            copy(block, block, z_s.at[step - 8, 4], z_r.at[step - 8, 4], sibling).wait_recv()
            share_copy(step - 8, 4).start()

        @pl.when(step == 13)
        def _():
            w_step(2)
            w_step(3)

        lax.fori_loop(first_unit(step), first_unit(step + 1), attend_unit, 0)
        return 0

    lax.fori_loop(0, 14, ring_step, 0)

    def finish(row, _):
        total = jnp.sum(l_ref[row], axis=1, keepdims=True)
        done = (acc_ref[row] / total).astype(jnp.bfloat16)
        own_att[0, row] = done[:ROWS]
        own_att[1, row] = done[ROWS:]
        return 0

    lax.fori_loop(0, NX, finish, 0)

    def g_slot(dx, dc, half):
        return att.at[2 * ((x + NX - dx) % NX) + (c + dc) % 2, 2 * half : 2 * half + 2]

    def g_copy(dx, dc, half):
        block = own_att.at[(c + dc) % 2, 2 * half : 2 * half + 2]
        return copy(
            block, g_slot(0, 0, half), g_s.at[dx, dc, half], g_r.at[dx, dc, half], device(dx, 0, dc)
        )

    def g_forward(dc, half):
        slot = g_slot(1 + 2 * half, dc, half)
        return copy(
            slot, slot, g_s.at[2, dc, half], g_r.at[2, dc, half], device(1 + 2 * half, 0, 0)
        )

    def g_arrival(dx, dc, half):
        slot = g_slot(dx, dc, half)
        return copy(slot, slot, g_s.at[dx, dc, half], g_r.at[dx, dc, half], sibling)

    onward = [(1, 0, 0), (3, 0, 1), (1, 1, 0), (3, 1, 1)]
    near = [(1, 0, 1), (3, 0, 0), (1, 1, 1), (3, 1, 0), (0, 1, 0), (0, 1, 1)]
    far = [(2, 0, 0), (2, 0, 1), (2, 1, 0), (2, 1, 1)]
    for place in onward + near:
        g_copy(*place).start()
    att[2 * x + c] = own_att[c]
    w_step(4)
    w_step(5)
    for dx, dc, half in onward:
        g_arrival(dx, dc, half).wait_recv()
        g_forward(dc, half).start()

    last_w = wbuf.at[(z + 4) % NZ, c]
    copy(last_w, last_w, w_s.at[4], w_r.at[4], sibling).wait_recv()
    w_share(4).start()

    for place in near + far:
        g_arrival(*place).wait_recv()

    def w_wait(r, _):
        w_share_arrival(r).wait_recv()
        return 0

    lax.fori_loop(0, NZ, w_wait, 0)

    def e_copy(row, nb):
        return copy(
            pbuf.at[row, nb], part.at[y, nb], e_s.at[row, nb], e_r.at[y, nb], (row * 16 + z * 2 + c, x)
        )

    def project(nb, _):
        left = jnp.concatenate([att[head].reshape(4 * ROWS, HD) for head in range(8)], axis=1)
        right = wbuf[pl.ds(2 * nb, 2)].reshape(2 * HD, 8 * HD)
        product = lax.dot_general(
            left, right, (((1,), (1,)), ((), ())), preferred_element_type=jnp.float32
        ).astype(jnp.bfloat16)
        for row in range(NX):
            pbuf[row, nb] = product[row * ROWS : (row + 1) * ROWS]
        for row in range(NX):
            mine = (x == row) & (y == x)

            @pl.when(mine)
            def _():
                part[y, nb] = pbuf[row, nb]

            @pl.when(jnp.logical_not(mine))
            def _():
                e_copy(row, nb).start()

        return 0

    lax.fori_loop(0, 4, project, 0)

    for dx in (1, 3, 2):
        x_copy(dx).wait_send()
    for dx, dc in partners:
        q_copy(dx, dc).wait_send()
    for place in onward + near:
        g_copy(*place).wait_send()
    for _, dc, half in far:
        g_forward(dc, half).wait_send()

    def sent(n, _):
        j = n % 4
        r = n // 4
        share_copy(j, r).wait_send()
        return 0

    lax.fori_loop(0, 32, sent, 0)

    def ring_sent(n, _):
        j = n % 4
        r = 1 + n // 4
        block = block_of(j, r)
        copy(block, block, z_s.at[j, r], z_r.at[j, r], sibling).wait_send()
        return 0

    lax.fori_loop(0, 28, ring_sent, 0)

    def w_sent(r, _):
        w_share(r).wait_send()
        return 0

    lax.fori_loop(0, NZ, w_sent, 0)

    def w_ring_sent(r, _):
        block = wbuf.at[(z + r) % NZ, c]
        copy(block, block, w_s.at[r], w_r.at[r], sibling).wait_send()
        return 0

    lax.fori_loop(1, NZ, w_ring_sent, 0)
    for nb in range(4):
        for source in range(NY):
            slot = part.at[source, nb]
            arrival = copy(slot, slot, e_s.at[source, nb], e_r.at[source, nb], sibling)

            @pl.when(jnp.logical_not((x == y) & (source == y)))
            def _():
                arrival.wait_recv()

        total = part[0, nb].astype(jnp.float32)
        for source in range(1, NY):
            total = total + part[source, nb].astype(jnp.float32)
        out_ref[:, nb * 256 : (nb + 1) * 256] = total.astype(jnp.bfloat16)

    for row in range(NX):
        mine = (x == row) & (y == x)

        @pl.when(jnp.logical_not(mine))
        def _():
            for nb in range(4):
                e_copy(row, nb).wait_send()


def shards(queries, keys, values, out_weight, doc_lengths):
    vmem = pl.BlockSpec(memory_space=pltpu.VMEM)
    hbm = pl.BlockSpec(memory_space=pltpu.HBM)
    bf16, f32 = jnp.bfloat16, jnp.float32
    dma = pltpu.SemaphoreType.DMA
    operands = (queries, keys, values, out_weight.T, jnp.asarray(frequencies()), doc_lengths)
    return pl.pallas_call(
        kernel,
        out_shape=jax.ShapeDtypeStruct((ROWS, 1024), bf16),
        in_specs=[hbm] * 6,
        out_specs=vmem,
        scratch_shapes=[
            pltpu.VMEM((1, HD), f32),
            pltpu.SMEM((6,), jnp.int32),
            pltpu.VMEM((ROWS, 1024), bf16),
            pltpu.VMEM((ROWS, 256), bf16),
            pltpu.VMEM((ROWS, 256), bf16),
            dma((6,)),
            pltpu.VMEM((8, ROWS, HD), bf16),
            pltpu.VMEM((2, 2, ROWS, HD), bf16),
            pltpu.VMEM((NX, 2, ROWS, HD), bf16),
            pltpu.VMEM((NX, NZ, 2, 2, ROWS, HD), bf16),
            pltpu.VMEM((NX, 2 * ROWS, HD), jnp.int32),
            pltpu.VMEM((NX, 2 * ROWS, HD), f32),
            pltpu.VMEM((NX, 2 * ROWS, HD), f32),
            pltpu.VMEM((NX, 2 * ROWS, HD), f32),
            pltpu.VMEM((2, NX, ROWS, HD), bf16),
            pltpu.VMEM((8, NX, ROWS, HD), bf16),
            pltpu.VMEM((NZ, 2, 64, 1024), bf16),
            pltpu.VMEM((NX, 4, ROWS, 256), bf16),
            pltpu.VMEM((NY, 4, ROWS, 256), bf16),
            dma((4,)), dma((4,)),
            dma((4, 2)), dma((4, 2)),
            dma((4, 8)), dma((4, 8)),
            dma((4, 8)), dma((4, 8)),
            dma((4, 2, 2)), dma((4, 2, 2)),
            dma((8,)), dma((8,)),
            dma((8,)), dma((8,)),
            dma((4, 4)), dma((4, 4)),
        ],
        compiler_params=pltpu.CompilerParams(
            collective_id=0, has_side_effects=True, vmem_limit_bytes=48 << 20
        ),
    )(*(pltpu.with_memory_space_constraint(array, pltpu.HBM) for array in operands))


def solution(mesh):
    in_specs = (P("tok", "feat"), P("tok", "feat"), P("tok", "feat"), P("feat", "tok"), P())
    return jax.shard_map(
        shards, mesh=mesh, in_specs=in_specs, out_specs=P("tok", "feat"), check_vma=False
    )
```
